256 devices in a mesh: gx: 64 (over z, y, core), gy: 4 (over x).
Axes of the slice: x: 4, y: 4, z: 8, core: 2. Of those that a mesh axis runs over, the one named last changes fastest.
Arguments:
- anomalies: float32 [131072, 1024], P(('gx', 'gy')), may hold values from -50 to 50
- obs_rows: int32 [64, 256], replicated, may hold values from 0 to 6143
- obs_var: float32 [64, 256], P('gx'), may hold values from 0.5 to 20
- taper_level: int32 [64, 3, 4], replicated, may hold values from 0 to 3
Outputs:
- posterior: float32 [131072, 1024], P(('gx', 'gy'))
The draws below stay inside these ranges and needn't reach their ends.
All inputs are finite; a program needn't handle non-finite values.
Results may differ from the reference program's by a relative error of at most 0.035.
The reference program's roundings to bfloat16 on the way count: a program that leaves them out, or rounds other values in their place, can miss the bound.
Values may be sent and summed in bfloat16 or wider, within the bound.
No kernel may reach another device: no remote copies, remote signals or barrier semaphores. Data moves between devices by JAX's collectives and lax.ppermute only.
A program may use at most 64 MiB of HBM per device.

```python
import math
import jax
import jax.numpy as jnp
from jax import lax

M = 1024
P_SIZE = 256
NCOL = 4
NS_STEPS = 12
ROWS_DEV = 512
NROWS = 131072
N_GX = 64
N_GY = 4


def draw_anomalies(key, part):
    first_key, second_key, third_key, fourth_key, fifth_key = jax.random.split(jax.random.fold_in(key, 17), 5)
    phase_shift = jax.random.uniform(fourth_key, (), jnp.float32, -math.pi, math.pi)
    angle_rows = 2.0 * math.pi / NROWS * jnp.arange(NROWS, dtype=jnp.float32)[:, None] + phase_shift
    values = jnp.clip(jax.random.normal(first_key, (NROWS, M), jnp.float32), -6.0, 6.0)
    row_scale = 0.3 * jnp.exp(jax.random.uniform(second_key, (NROWS, 1), jnp.float32, 0.0, math.log(10.0)))
    factors = jnp.clip(jax.random.normal(fifth_key, (2, M), jnp.float32), -2.5, 2.5)
    loading = 1.5
    column_scale = 0.5 * jnp.exp(jax.random.uniform(third_key, (1, M), jnp.float32, 0.0, math.log(4.0)))
    common = loading * (jnp.cos(angle_rows) * factors[0][None, :] + jnp.sin(angle_rows) * factors[1][None, :])
    return jnp.clip(row_scale * (values * column_scale + common), -49.0, 49.0).astype(jnp.float32)


def place_ends(array, own_key, least, high):
    extent = array.shape
    spot = [jax.random.randint(jax.random.fold_in(own_key, axis), (), 0, extent[axis]) for axis in range(len(extent))]
    array = array.at[tuple(spot)].set(least)
    longest = extent.index(max(extent))
    spot[longest] = (spot[longest] + 1) % extent[longest]
    return array.at[tuple(spot)].set(high)


def block_levels(own_key, shape, cuts, least, largest):
    gain = 1.0
    for axis_at, shards_of in cuts:
        draws = jax.random.uniform(jax.random.fold_in(jax.random.fold_in(own_key, 6), axis_at), (shards_of,), jnp.float32, least / len(cuts), largest / len(cuts))
        gain = gain * jnp.repeat(jnp.exp(draws), shape[axis_at] // shards_of).reshape((-1,) + (1,) * (len(shape) - 1 - axis_at))
    return gain


def setup_inputs(seed: int = 0) -> dict:
    arg_keys = jax.random.split(jax.random.key(seed), 5)
    return {
        "anomalies": draw_anomalies(jax.random.fold_in(arg_keys[4], 71), 0),
        "obs_rows": place_ends(jax.random.randint(arg_keys[1], (N_GX, P_SIZE), 0, 3 * N_GY * ROWS_DEV), jax.random.fold_in(arg_keys[1], 1), 0, (3 * N_GY * ROWS_DEV) - 1).astype(jnp.int32),
        "obs_var": jnp.clip(jnp.exp(math.log(20.0) - 3.6888795 * jax.random.uniform(arg_keys[2], (N_GX, P_SIZE), jnp.float32) ** block_levels(arg_keys[2], (N_GX, P_SIZE), ((0, 64),), -0.2, 0.2)), 0.5, 20.0),
        "taper_level": place_ends(jax.random.randint(arg_keys[3], (N_GX, 3, N_GY), 0, 4), jax.random.fold_in(arg_keys[3], 1), 0, 3).astype(jnp.int32),
    }


def mat_prod(left, right):
    return jnp.dot(left, right, precision=lax.Precision.HIGHEST, preferred_element_type=jnp.float32)

def region_rows(batch):
    columns = (batch - 1 + jnp.arange(3, dtype=jnp.int32)) % N_GX
    inside = jnp.arange(N_GY * ROWS_DEV, dtype=jnp.int32)
    return (columns[:, None] * (N_GY * ROWS_DEV) + inside[None, :]).reshape(-1).astype(jnp.int32)

def inverse_root(gram_matrix):
    identity_mat = jnp.eye(gram_matrix.shape[0], dtype=jnp.float32)
    trace_value = jnp.trace(gram_matrix)
    iter_left = gram_matrix / trace_value
    iter_right = identity_mat
    for sweep in range(NS_STEPS):
        newton_term = 1.5 * identity_mat - 0.5 * mat_prod(iter_right, iter_left)
        iter_left = mat_prod(iter_left, newton_term)
        iter_right = mat_prod(newton_term, iter_right)
    return iter_right / jnp.sqrt(trace_value)

def reference(anomalies, obs_rows, obs_var, taper_level):
    state_now = anomalies
    for colour in range(NCOL):
        batch_ids = (colour + NCOL * jnp.arange(N_GX // NCOL, dtype=jnp.int32)).astype(jnp.int32)

        def update_one(batch):
            row_ids = region_rows(batch)
            region_state = state_now[row_ids]
            observed = region_state[obs_rows[batch]].astype(jnp.bfloat16)
            gram_matrix = jnp.dot(observed, observed.T, preferred_element_type=jnp.float32) / (M - 1) + jnp.diag(obs_var[batch])
            inverse_half = inverse_root(gram_matrix).astype(jnp.bfloat16)
            transformed = jnp.dot(inverse_half, observed, preferred_element_type=jnp.float32).astype(jnp.bfloat16)
            projected = jnp.dot(region_state.astype(jnp.bfloat16), transformed.T, preferred_element_type=jnp.float32).astype(jnp.bfloat16)
            increment = jnp.dot(projected, transformed, preferred_element_type=jnp.float32)
            tapering = jnp.repeat(taper_level[batch].reshape(-1).astype(jnp.float32) / 3.0, ROWS_DEV)
            return (region_state - (tapering / (M - 1))[:, None] * increment, row_ids)
        updated, row_ids = lax.map(update_one, batch_ids)
        state_now = state_now.at[row_ids.reshape(-1)].set(updated.reshape(-1, M))
    return state_now
```

```python
import functools

import jax
import jax.numpy as jnp
from jax import lax
from jax.experimental import pallas as pl
from jax.experimental.pallas import tpu as pltpu
from jax.sharding import PartitionSpec as P

NCOL = 4
NS_STEPS = 12
LEAD = 2
AXES = ("gx", "gy")
VMEM_LIMIT = 20 << 20
INTERPRET = False
F32 = jnp.float32
BF16 = jnp.bfloat16


def kernel_call(body, out, args, name, flops, smem=()):
    whole = pl.BlockSpec(memory_space=pltpu.VMEM)
    scalar = pl.BlockSpec(memory_space=pltpu.SMEM)
    leaves = [*args, *jax.tree.leaves(out)]
    return pl.pallas_call(
        body,
        out_shape=out,
        in_specs=[scalar if n in smem else whole for n in range(len(args))],
        out_specs=jax.tree.map(lambda _: whole, out),
        name=name,
        interpret=INTERPRET,
        cost_estimate=pl.CostEstimate(
            flops=flops,
            bytes_accessed=sum(leaf.size * leaf.dtype.itemsize for leaf in leaves),
            transcendentals=0,
        ),
        compiler_params=pltpu.CompilerParams(vmem_limit_bytes=VMEM_LIMIT),
    )(*args)


def dot(left, right):
    return jnp.dot(left, right, preferred_element_type=F32)


def dot_nt(left, right):
    return lax.dot_general(
        left, right, (((1,), (1,)), ((), ())), preferred_element_type=F32
    )


def halves(value):
    high = value.astype(BF16)
    return high, (value - high.astype(F32)).astype(BF16)


def mat_prod(left, right):
    return dot(left[0], right[0]) + (dot(left[0], right[1]) + dot(left[1], right[0]))


def pick_kernel(state, index, *outs):
    rows = outs[0].shape[0]
    spots = lax.broadcasted_iota(jnp.int32, (len(outs) * rows, state.shape[0]), 1)
    chosen = jnp.where(spots == index[...], 1.0, 0.0).astype(BF16)
    rest = state[...]
    high = rest.astype(BF16)
    picked = dot(chosen, high)
    if outs[0].dtype == F32:
        rest = rest - high.astype(F32)
        middle = rest.astype(BF16)
        low = (rest - middle.astype(F32)).astype(BF16)
        picked = (picked + dot(chosen, middle)) + dot(chosen, low)
    for n, out in enumerate(outs):
        out[...] = picked[n * rows : (n + 1) * rows].astype(out.dtype)


def root_kernel(*refs):
    *pieces, variance, out = refs
    observed = jnp.concatenate([piece[...] for piece in pieces], axis=0)
    size, members = observed.shape
    row = lax.broadcasted_iota(jnp.int32, (size, size), 0)
    column = lax.broadcasted_iota(jnp.int32, (size, size), 1)
    eye = jnp.where(row == column, 1.0, 0.0).astype(F32)
    gram = dot_nt(observed, observed) / (members - 1) + eye * variance[...]
    trace = jnp.sum(jnp.sum(gram * eye, axis=1, keepdims=True), axis=0, keepdims=True)
    left = gram / trace
    term = 1.5 * eye - 0.5 * left
    right = term
    left_h, term_h = halves(left), halves(term)
    right_h = term_h
    left_h = halves(mat_prod(left_h, term_h))
    for sweep in range(1, NS_STEPS):
        term_h = halves(1.5 * eye - 0.5 * mat_prod(right_h, left_h))
        if sweep < NS_STEPS - 1:
            left_h = halves(mat_prod(left_h, term_h))
        right = mat_prod(term_h, right_h)
        if sweep < NS_STEPS - 1:
            right_h = halves(right)
    inverse_half = (right / jnp.sqrt(trace)).astype(BF16)
    out[...] = dot(inverse_half, observed).astype(BF16)


def stepped(rows, factor, transformed):
    projected = dot_nt(rows.astype(BF16), transformed).astype(BF16)
    return rows - factor * dot(projected, transformed)


def rows_kernel(count, *refs):
    rows, transformed, factors = refs[0], refs[1 : 1 + count], refs[1 + count : 1 + 2 * count]
    value = rows[...]
    for source, factor in zip(transformed, factors):
        value = stepped(value, factor[...], source[...])
    for out in refs[1 + 2 * count :]:
        out[...] = value.astype(out.dtype)


def tile_kernel(count, own, *refs):
    state, scalars, sources, out = refs[0], refs[1], refs[2 : 2 + count], refs[2 + count]
    got = sources[0][...]
    for source in sources[1:]:
        got = got + source[...]
    if own:
        got = jnp.where(scalars[0, 1] > 0.5, refs[2 + count][...], got)
        out = refs[3 + count]
    out[...] = stepped(state[...], scalars[0, 0], got)


def on_device(anomalies, obs_rows, obs_var, taper_level):
    tile_rows, members = anomalies.shape
    batches, size = obs_rows.shape
    columns = lax.axis_size("gx")
    tiles = lax.axis_size("gy")
    share = size // tiles
    col = lax.axis_index("gx")
    tile = lax.axis_index("gy")
    kind = col % NCOL
    lead_batch = col - LEAD
    is_lead = kind == LEAD
    leaders = range(LEAD, columns, NCOL)

    def hop(value, pairs):
        flat = [
            ((a % columns) * tiles + b % tiles, (c % columns) * tiles + d % tiles)
            for (a, b), (c, d) in pairs
        ]
        return lax.ppermute(value, AXES, flat)

    def along_gx(value, from_lead, to_lead):
        pairs = [
            ((lead + from_lead, n), (lead + to_lead, n))
            for lead in leaders
            for n in range(tiles)
        ]
        return hop(value, pairs)

    def along_gy(value, kept, step):
        pairs = [((c, n), (c, n + step)) for c in kept for n in range(tiles)]
        return hop(value, pairs)

    def region_slot(colour):
        offset = (col - colour) % NCOL
        slot = jnp.where(offset == 1, 2, jnp.where(offset == 3, 0, 1)).astype(jnp.int32)
        return slot, offset != 2, (col - slot + 1) % columns

    def local_index(colour):
        slot, active, batch = region_slot(colour)
        local = obs_rows[batch] - (slot * tiles + tile) * tile_rows
        local = jnp.where(active, local, -1)
        return jnp.roll(local, -share * tile)[:, None]

    def pick(colour, dtype):
        return kernel_call(
            pick_kernel,
            [jax.ShapeDtypeStruct((share, members), dtype)] * tiles,
            [anomalies, local_index(colour)],
            "pick",
            2 * size * tile_rows * members * (1 if dtype == BF16 else 3),
        )

    def gathered(colour, parts):
        kept = [c for c in range(columns) if (c - colour) % NCOL != 2]
        total = parts[0]
        for step in range(1, tiles):
            total = total + along_gy(parts[step], kept, step)
        whole = total
        for place in range(colour - LEAD - 1, colour - LEAD + 2):
            if place != 0:
                whole = whole + along_gx(total, place, 0)
        return whole

    def variance_of(colour):
        place = colour - LEAD
        value = obs_var if place == 0 else along_gx(obs_var, place, 0)
        value = jnp.where(is_lead, value, 1.0)
        pieces = value.reshape(tiles, share)
        order = (tile - jnp.arange(tiles)) % tiles
        return jnp.take(pieces, order, axis=0).reshape(1, size)

    def row_factor(target, source):
        picked = lax.dynamic_slice_in_dim(
            obs_rows[(lead_batch + target) % batches], tile * share, share
        )
        slot = picked // (tiles * tile_rows) + (target - source)
        place = slot * tiles + (picked // tile_rows) % tiles
        levels = taper_level[(lead_batch + source) % batches].reshape(-1).astype(F32) / 3.0
        factors = levels / (members - 1)
        spots = jnp.arange(3 * tiles, dtype=jnp.int32)
        hit = (place[:, None] == spots[None, :]) & (slot >= 0)[:, None]
        return jnp.sum(jnp.where(hit, factors[None, :], 0.0), axis=1, keepdims=True)

    def move_rows(rows, sources, with_bf16):
        outs = [jax.ShapeDtypeStruct(rows.shape, BF16 if with_bf16 else F32)]
        args = [rows, *[t for t, _ in sources], *[f for _, f in sources]]
        return kernel_call(
            functools.partial(rows_kernel, len(sources)),
            outs,
            args,
            "rows",
            4 * rows.shape[0] * size * members * len(sources),
        )[0]

    def spread(rows):
        kept = list(leaders)
        return [rows, *[along_gy(rows, kept, step) for step in range(1, tiles)]]

    def transform(rows, variance):
        pieces = spread(rows)
        return kernel_call(
            root_kernel,
            jax.ShapeDtypeStruct((size, members), BF16),
            [*pieces, variance],
            "root",
            8_000_000_000,
        )

    def move_tile(state, colour, transformed, received):
        slot, active, batch = region_slot(colour)
        level = taper_level[batch, slot, tile].astype(F32) / 3.0
        factor = jnp.where(active, level, 0.0) / (members - 1)
        own = colour - LEAD in (-1, 0, 1)
        scalars = jnp.stack([factor, is_lead.astype(F32)]).reshape(1, 2)
        return kernel_call(
            functools.partial(tile_kernel, len(received), own),
            jax.ShapeDtypeStruct(state.shape, F32),
            [state, scalars, *received, *([transformed] if own else [])],
            "tile",
            4 * tile_rows * size * members,
            smem=(1,),
        )

    def deliver(colour, transformed):
        places = range(colour - LEAD - 1, colour - LEAD + 2)
        return [along_gx(transformed, 0, place) for place in places if place != 0]

    variances = [variance_of(colour) for colour in range(NCOL)]
    first = gathered(0, pick(0, BF16))
    rows = [None] + [gathered(colour, pick(colour, F32)) for colour in range(1, NCOL)]

    t0 = transform(first, variances[0])
    u0 = along_gx(t0, 0, -NCOL)
    got0 = deliver(0, t0)
    next1 = move_rows(rows[1], [(t0, row_factor(1, 0))], True)
    rows2 = move_rows(rows[2], [(t0, row_factor(2, 0))], False)
    t1 = transform(next1, variances[1])
    u1 = along_gx(t1, 0, -NCOL)
    got1 = deliver(1, t1)
    next2 = move_rows(rows2, [(t1, row_factor(2, 1)), (u0, row_factor(2, 4))], True)
    rows3 = move_rows(rows[3], [(u0, row_factor(3, 4)), (t1, row_factor(3, 1))], False)
    t2 = transform(next2, variances[2])
    got2 = deliver(2, t2)
    next3 = move_rows(rows3, [(u1, row_factor(3, 5)), (t2, row_factor(3, 2))], True)
    t3 = transform(next3, variances[3])
    got3 = deliver(3, t3)

    state = move_tile(anomalies, 0, t0, got0)
    state = move_tile(state, 1, t1, got1)
    state = move_tile(state, 2, t2, got2)
    return move_tile(state, 3, t3, got3)


def solution(mesh):
    in_specs = (P(AXES, None), P(), P("gx", None), P())
    return jax.shard_map(
        on_device,
        mesh=mesh,
        in_specs=in_specs,
        out_specs=P(AXES, None),
        check_vma=False,
    )
```

```python
import functools

import jax
import jax.numpy as jnp
from jax import lax
from jax.experimental import pallas as pl
from jax.experimental.pallas import tpu as pltpu
from jax.sharding import PartitionSpec as P

NCOL = 4
NS_STEPS = 12
AXES = ("gx", "gy")
VMEM_LIMIT = 20 << 20
INTERPRET = False
F32 = jnp.float32
BF16 = jnp.bfloat16


def kernel_call(body, out, args, name, flops, smem=(), scratch=()):
    whole = pl.BlockSpec(memory_space=pltpu.VMEM)
    scalar = pl.BlockSpec(memory_space=pltpu.SMEM)
    leaves = [*args, *jax.tree.leaves(out)]
    return pl.pallas_call(
        body,
        out_shape=out,
        in_specs=[scalar if n in smem else whole for n in range(len(args))],
        out_specs=jax.tree.map(lambda _: whole, out),
        scratch_shapes=scratch,
        name=name,
        interpret=INTERPRET,
        cost_estimate=pl.CostEstimate(
            flops=flops,
            bytes_accessed=sum(leaf.size * leaf.dtype.itemsize for leaf in leaves),
            transcendentals=0,
        ),
        compiler_params=pltpu.CompilerParams(vmem_limit_bytes=VMEM_LIMIT),
    )(*args)


def dot(left, right):
    return jnp.dot(left, right, preferred_element_type=F32)


def dot_nt(left, right):
    return lax.dot_general(
        left, right, (((1,), (1,)), ((), ())), preferred_element_type=F32
    )


def dot_tn(left, right):
    return lax.dot_general(
        left, right, (((0,), (0,)), ((), ())), preferred_element_type=F32
    )


def halves(value):
    high = value.astype(BF16)
    return high, (value - high.astype(F32)).astype(BF16)


def mat_prod(left, right):
    return dot(left[0], right[0]) + (dot(left[0], right[1]) + dot(left[1], right[0]))


def standing(col, colour, columns):
    offset = lax.rem(col + (NCOL - colour), NCOL)
    slot = jnp.where(offset == 1, 2, jnp.where(offset == 3, 0, 1))
    return slot, offset != 2, lax.rem(col - slot + 1 + columns, columns)


def pick_kernel(colours, state, obs, place, *refs):
    outs, scratch = refs[:-1], refs[-1]
    tiles = len(outs)
    tile_rows = state.shape[0]
    columns, size = obs.shape
    share = size // tiles
    col, tile = place[0, 0], place[0, 1]
    rest = state[...]
    parts = [rest.astype(BF16)]
    if outs[0].dtype == F32:
        rest = rest - parts[0].astype(F32)
        parts.append(rest.astype(BF16))
        parts.append((rest - parts[1].astype(F32)).astype(BF16))
    for n, colour in enumerate(colours):
        slot, active, batch = standing(col, colour, columns)
        first = jnp.where(active, (slot * tiles + tile) * tile_rows, -(1 << 20))
        local = obs[pl.ds(batch, 1), :] - first
        spots = lax.broadcasted_iota(jnp.int32, (tile_rows, size), 0)
        chosen = jnp.where(spots == local, 1.0, 0.0).astype(BF16)
        picked = dot_tn(chosen, parts[0])
        for part in parts[1:]:
            picked = picked + dot_tn(chosen, part)
        scratch[...] = picked.astype(scratch.dtype)
        for step, out in enumerate(outs):
            start = pl.multiple_of(lax.rem(tile + step, tiles) * share, share)
            out[n * share : (n + 1) * share, :] = scratch[pl.ds(start, share), :]


def setup_kernel(pairs, tiles, tile_rows, obs, levels, place, own, left, right, *outs):
    columns, size = obs.shape
    share = size // tiles
    col, tile = place[0, 0], place[0, 1]
    members = place[0, 2].astype(F32)
    lane = lax.broadcasted_iota(jnp.int32, (share, size), 1)
    mine = lane == lax.broadcasted_iota(jnp.int32, (share, size), 0) + tile * share

    def factor(source, which):
        slot, active, batch = standing(col, source, columns)
        level = levels[batch, slot * tiles + which].astype(F32) / 3.0
        return jnp.where(active, level, 0.0)

    for (targets, source), out in zip(pairs, outs):
        for n, target in enumerate(targets):
            slot, _, batch = standing(col, target, columns)
            inside = obs[pl.ds(batch, 1), :] - slot * (tiles * tile_rows)
            row = jnp.zeros((1, size), F32)
            for which in range(tiles):
                hit = (inside >= which * tile_rows) & (inside < (which + 1) * tile_rows)
                row = jnp.where(hit, factor(source, which), row)
            column = jnp.sum(jnp.where(mine, row, 0.0), axis=1, keepdims=True)
            out[n * share : (n + 1) * share, :] = column / members
    for colour in range(NCOL):
        outs[len(pairs) + colour][...] = jnp.full((1, 1), factor(colour, tile)) / members
        slot, active, _ = standing(col, colour, columns)
        value = jnp.where(
            active & (slot == 2), left[...], jnp.where(active & (slot == 0), right[...], own[...])
        )
        pieces = [value[:, n * share : (n + 1) * share] for n in range(tiles)]
        ordered = []
        for step in range(tiles):
            source = lax.rem(tile + tiles - step, tiles)
            piece = pieces[0]
            for n in range(1, tiles):
                piece = jnp.where(source == n, pieces[n], piece)
            ordered.append(piece)
        outs[len(pairs) + NCOL + colour][...] = jnp.concatenate(ordered, axis=1)


def root_kernel(*refs):
    *pieces, variance, out = refs
    observed = jnp.concatenate([piece[...] for piece in pieces], axis=0)
    size, members = observed.shape
    row = lax.broadcasted_iota(jnp.int32, (size, size), 0)
    column = lax.broadcasted_iota(jnp.int32, (size, size), 1)
    eye = jnp.where(row == column, 1.0, 0.0).astype(F32)
    gram = dot_nt(observed, observed) / (members - 1) + eye * variance[...]
    trace = jnp.sum(jnp.sum(gram * eye, axis=1, keepdims=True), axis=0, keepdims=True)
    left = gram / trace
    right_h = halves(1.5 * eye - 0.5 * left)
    left_h = halves(mat_prod(halves(left), right_h))

    def next_term(left_h, right_h):
        return halves(1.5 * eye - 0.5 * mat_prod(right_h, left_h))

    def step(_, pair):
        left_h, right_h = pair
        term_h = next_term(left_h, right_h)
        return halves(mat_prod(left_h, term_h)), halves(mat_prod(term_h, right_h))

    left_h, right_h = lax.fori_loop(1, NS_STEPS - 1, step, (left_h, right_h))
    right = mat_prod(next_term(left_h, right_h), right_h)
    inverse_half = (right / jnp.sqrt(trace)).astype(BF16)
    out[...] = dot(inverse_half, observed).astype(BF16)


def rows_kernel(count, *refs):
    parts, transformed, factor, outs = refs[:count], refs[count], refs[count + 1], refs[count + 2 :]
    rows = parts[0][...]
    for part in parts[1:]:
        rows = rows + part[...]
    source = transformed[...]
    projected = dot_nt(rows.astype(BF16), source).astype(BF16)
    rows = rows - factor[...] * dot(projected, source)
    share = outs[0].shape[0]
    for n, out in enumerate(outs):
        out[...] = rows[n * share : (n + 1) * share].astype(out.dtype)


def sum_kernel(*refs):
    *parts, out = refs
    total = parts[0][...]
    for part in parts[1:]:
        total = total + part[...]
    out[...] = total


def on_device(anomalies, obs_rows, obs_var, taper_level):
    tile_rows, members = anomalies.shape
    batches, size = obs_rows.shape
    columns = lax.axis_size("gx")
    tiles = lax.axis_size("gy")
    share = size // tiles
    col = lax.axis_index("gx")
    tile = lax.axis_index("gy")
    place = jnp.stack([col, tile, jnp.int32(members - 1)]).astype(jnp.int32).reshape(1, 3)
    levels = taper_level.reshape(batches, 3 * tiles)
    everywhere = list(range(columns))

    def kept_of(colour):
        return [c for c in everywhere if (c - colour) % NCOL != 2]

    def hop(value, pairs):
        flat = [
            ((a % columns) * tiles + b % tiles, (c % columns) * tiles + d % tiles)
            for (a, b), (c, d) in pairs
        ]
        return lax.ppermute(value, AXES, flat)

    def along_gy(value, kept, step):
        return hop(value, [((c, n), (c, n + step)) for c in kept for n in range(tiles)])

    def along_gx(value, colour, step):
        trio = (-1, 0, 1)
        pairs = [
            ((b + trio[m], n), (b + trio[(m + step) % 3], n))
            for b in range(colour, columns, NCOL)
            for m in range(3)
            for n in range(tiles)
        ]
        return hop(value, pairs)

    def beside(value, step):
        return hop(value, [((c, n), (c + step, n)) for c in everywhere for n in range(tiles)])

    def pick(colours, dtype, state):
        shape = jax.ShapeDtypeStruct((len(colours) * share, members), dtype)
        return kernel_call(
            functools.partial(pick_kernel, colours),
            [shape] * tiles,
            [state, obs_rows, place],
            "pick",
            2 * size * tile_rows * members * len(colours) * (1 if dtype == BF16 else 3),
            smem=(2,),
            scratch=[pltpu.VMEM((size, members), dtype)],
        )

    def scattered(parts, kept):
        return [parts[0], *[along_gy(parts[n], kept, n) for n in range(1, tiles)]]

    def added(parts):
        return kernel_call(
            sum_kernel,
            jax.ShapeDtypeStruct(parts[0].shape, parts[0].dtype),
            parts,
            "sum",
            1_000_000,
        )

    def collected(rows, colour):
        whole = added([rows, along_gx(rows, colour, 1), along_gx(rows, colour, 2)])
        kept = kept_of(colour)
        return [whole, *[along_gy(whole, kept, step) for step in range(1, tiles)]]

    def transform(pieces, variance):
        return kernel_call(
            root_kernel,
            jax.ShapeDtypeStruct((size, members), BF16),
            [*pieces, variance],
            "root",
            8_000_000_000,
        )

    def move(parts, transformed, factor, dtypes, name="rows"):
        rows = parts[0].shape[0]
        shape = (rows // len(dtypes), members)
        return kernel_call(
            functools.partial(rows_kernel, len(parts)),
            [jax.ShapeDtypeStruct(shape, dtype) for dtype in dtypes],
            [*parts, transformed, factor],
            name,
            4 * rows * size * members,
        )

    together = lax.optimization_barrier
    parts0 = scattered(pick((0,), BF16, anomalies), kept_of(0))
    total0 = added(parts0)
    picked1 = pick((1,), F32, anomalies)
    picked23 = pick((2, 3), F32, anomalies)

    pairs = (((1,), 0), ((2, 3), 0), ((2,), 1), ((3,), 1), ((3,), 2))
    own_var, _ = together((obs_var, total0))
    prepared = kernel_call(
        functools.partial(setup_kernel, pairs, tiles, tile_rows),
        [jax.ShapeDtypeStruct((len(t) * share, 1), F32) for t, _ in pairs]
        + [jax.ShapeDtypeStruct((1, 1), F32)] * NCOL
        + [jax.ShapeDtypeStruct((1, size), F32)] * NCOL,
        [obs_rows, levels, place, obs_var, beside(own_var, 1), beside(own_var, -1)],
        "setup",
        1_000_000,
        smem=(1, 2),
    )
    f10, f230, f21, f31, f32_ = prepared[: len(pairs)]
    tile_factor = prepared[len(pairs) : len(pairs) + NCOL]
    variance = prepared[len(pairs) + NCOL :]

    picked1, total0 = together((picked1, total0))
    parts1 = scattered(picked1, kept_of(1))
    pieces = collected(total0, 0)
    picked23, pieces = together((picked23, pieces))
    parts23 = scattered(picked23, everywhere)
    t0 = transform(pieces, variance[0])

    (next1,) = move(parts1, t0, f10, [BF16])
    (state,) = move([anomalies], t0, tile_factor[0], [F32], "tile")
    pieces = collected(next1, 1)
    var1, state = together((variance[1], state))
    t1 = transform(pieces, var1)

    rows2, rows3 = move(parts23, t0, f230, [F32, F32])
    (next2,) = move([rows2], t1, f21, [BF16])
    (rows3,) = move([rows3], t1, f31, [F32])
    (state,) = move([state], t1, tile_factor[1], [F32], "tile")
    pieces = collected(next2, 2)
    var2, state, rows3 = together((variance[2], state, rows3))
    t2 = transform(pieces, var2)

    (next3,) = move([rows3], t2, f32_, [BF16])
    (state,) = move([state], t2, tile_factor[2], [F32], "tile")
    pieces = collected(next3, 3)
    var3, state = together((variance[3], state))
    t3 = transform(pieces, var3)
    (state,) = move([state], t3, tile_factor[3], [F32], "tile")
    return state


def solution(mesh):
    in_specs = (P(AXES, None), P(), P("gx", None), P())
    return jax.shard_map(
        on_device,
        mesh=mesh,
        in_specs=in_specs,
        out_specs=P(AXES, None),
        check_vma=False,
    )
```

```python
import functools

import jax
import jax.numpy as jnp
from jax import lax
from jax.experimental import pallas as pl
from jax.experimental.pallas import tpu as pltpu
from jax.sharding import PartitionSpec as P

NCOL = 4
NS_STEPS = 12
AXES = ("gx", "gy")
VMEM_LIMIT = 20 << 20
INTERPRET = False
F32 = jnp.float32
BF16 = jnp.bfloat16


def kernel_call(body, out, args, name, flops, smem=()):
    whole = pl.BlockSpec(memory_space=pltpu.VMEM)
    scalar = pl.BlockSpec(memory_space=pltpu.SMEM)
    leaves = [*args, *jax.tree.leaves(out)]
    return pl.pallas_call(
        body,
        out_shape=out,
        in_specs=[scalar if n in smem else whole for n in range(len(args))],
        out_specs=jax.tree.map(lambda _: whole, out),
        name=name,
        interpret=INTERPRET,
        cost_estimate=pl.CostEstimate(
            flops=flops,
            bytes_accessed=sum(leaf.size * leaf.dtype.itemsize for leaf in leaves),
            transcendentals=0,
        ),
        compiler_params=pltpu.CompilerParams(vmem_limit_bytes=VMEM_LIMIT),
    )(*args)


def dot(left, right):
    return jnp.dot(left, right, preferred_element_type=F32)


def dot_nt(left, right):
    return lax.dot_general(
        left, right, (((1,), (1,)), ((), ())), preferred_element_type=F32
    )


def dot_tn(left, right):
    return lax.dot_general(
        left, right, (((0,), (0,)), ((), ())), preferred_element_type=F32
    )


def halves(value):
    high = value.astype(BF16)
    return high, (value - high.astype(F32)).astype(BF16)


def mat_prod(left, right):
    return dot(left[0], right[0]) + (dot(left[0], right[1]) + dot(left[1], right[0]))


def standing(col, colour, columns):
    offset = lax.rem(col + (NCOL - colour), NCOL)
    slot = jnp.where(offset == 1, 2, jnp.where(offset == 3, 0, 1))
    return slot, offset != 2, lax.rem(col - slot + 1 + columns, columns)


def pick_kernel(tiles, colours, state, obs, place, out):
    tile_rows = state.shape[0]
    columns, size = obs.shape
    share = size // tiles
    col, tile = place[0, 0], place[0, 1]
    rest = state[...]
    parts = [rest.astype(BF16)]
    if out.dtype == F32:
        rest = rest - parts[0].astype(F32)
        parts.append(rest.astype(BF16))
        parts.append((rest - parts[1].astype(F32)).astype(BF16))
    for n, colour in enumerate(colours):
        slot, active, batch = standing(col, colour, columns)
        first = jnp.where(active, (slot * tiles + tile) * tile_rows, -(1 << 20))
        local = obs[pl.ds(batch, 1), :] - first
        spots = lax.broadcasted_iota(jnp.int32, (tile_rows, size), 0)
        chosen = jnp.where(spots == local, 1.0, 0.0).astype(BF16)
        picked = dot_tn(chosen, parts[0])
        for part in parts[1:]:
            picked = picked + dot_tn(chosen, part)
        picked = picked.astype(out.dtype)
        for m in range(tiles):
            start = (m * len(colours) + n) * share
            out[start : start + share, :] = picked[m * share : (m + 1) * share]


def setup_kernel(pairs, tiles, tile_rows, obs, levels, place, own, left, right, *outs):
    columns, size = obs.shape
    share = size // tiles
    col, tile = place[0, 0], place[0, 1]
    members = place[0, 2].astype(F32)
    lane = lax.broadcasted_iota(jnp.int32, (share, size), 1)
    mine = lane == lax.broadcasted_iota(jnp.int32, (share, size), 0) + tile * share

    def factor(source, which):
        slot, active, batch = standing(col, source, columns)
        level = levels[batch, slot * tiles + which].astype(F32) / 3.0
        return jnp.where(active, level, 0.0)

    for (targets, source), out in zip(pairs, outs):
        for n, target in enumerate(targets):
            slot, _, batch = standing(col, target, columns)
            inside = obs[pl.ds(batch, 1), :] - slot * (tiles * tile_rows)
            row = jnp.zeros((1, size), F32)
            for which in range(tiles):
                hit = (inside >= which * tile_rows) & (inside < (which + 1) * tile_rows)
                row = jnp.where(hit, factor(source, which), row)
            column = jnp.sum(jnp.where(mine, row, 0.0), axis=1, keepdims=True)
            out[n * share : (n + 1) * share, :] = column / members
    for colour in range(NCOL):
        outs[len(pairs) + colour][...] = jnp.full((1, 1), factor(colour, tile)) / members
        slot, active, _ = standing(col, colour, columns)
        value = jnp.where(
            active & (slot == 2), left[...], jnp.where(active & (slot == 0), right[...], own[...])
        )
        outs[len(pairs) + NCOL + colour][...] = value


def root_kernel(pieces, variance, out):
    observed = pieces[...]
    size, members = observed.shape
    row = lax.broadcasted_iota(jnp.int32, (size, size), 0)
    column = lax.broadcasted_iota(jnp.int32, (size, size), 1)
    eye = jnp.where(row == column, 1.0, 0.0).astype(F32)
    gram = dot_nt(observed, observed) / (members - 1) + eye * variance[...]
    trace = jnp.sum(jnp.sum(gram * eye, axis=1, keepdims=True), axis=0, keepdims=True)
    left = gram / trace
    right_h = halves(1.5 * eye - 0.5 * left)
    left_h = halves(mat_prod(halves(left), right_h))

    def next_term(left_h, right_h):
        return halves(1.5 * eye - 0.5 * mat_prod(right_h, left_h))

    def step(_, pair):
        left_h, right_h = pair
        term_h = next_term(left_h, right_h)
        return halves(mat_prod(left_h, term_h)), halves(mat_prod(term_h, right_h))

    left_h, right_h = lax.fori_loop(1, NS_STEPS - 1, step, (left_h, right_h))
    right = mat_prod(next_term(left_h, right_h), right_h)
    inverse_half = (right / jnp.sqrt(trace)).astype(BF16)
    out[...] = dot(inverse_half, observed).astype(BF16)


def summed(parts, count):
    rows = parts.shape[0] // count
    total = parts[:rows, :]
    for n in range(1, count):
        total = total + parts[n * rows : (n + 1) * rows, :]
    return total


def rows_kernel(count, parts, *refs):
    *pairs, out = refs
    rows = summed(parts, count)
    for transformed, factor in zip(pairs[::2], pairs[1::2]):
        source = transformed[...]
        projected = dot_nt(rows.astype(BF16), source).astype(BF16)
        rows = rows - factor[...] * dot(projected, source)
    out[...] = rows.astype(out.dtype)


def sum_kernel(count, parts, out):
    out[...] = summed(parts, count)


def copies_kernel(own, first, second, out):
    total = (own[...] + first[...]) + second[...]
    rows = total.shape[0]
    for n in range(out.shape[0] // rows):
        out[n * rows : (n + 1) * rows, :] = total


def on_device(anomalies, obs_rows, obs_var, taper_level):
    tile_rows, members = anomalies.shape
    batches, size = obs_rows.shape
    columns = lax.axis_size("gx")
    tiles = lax.axis_size("gy")
    share = size // tiles
    col = lax.axis_index("gx")
    tile = lax.axis_index("gy")
    place = jnp.stack([col, tile, jnp.int32(members - 1)]).astype(jnp.int32).reshape(1, 3)
    levels = taper_level.reshape(batches, 3 * tiles)
    everywhere = list(range(columns))

    def hop(value, pairs):
        flat = [
            ((a % columns) * tiles + b % tiles, (c % columns) * tiles + d % tiles)
            for (a, b), (c, d) in pairs
        ]
        return lax.ppermute(value, AXES, flat)

    def over_gy(value):
        rows = value.shape[0]
        parts = value.reshape(tiles, rows // tiles, members)
        return lax.all_to_all(parts, "gy", 0, 0, tiled=True).reshape(rows, members)

    def along_gx(value, colour, step):
        trio = (-1, 0, 1)
        pairs = [
            ((b + trio[m], n), (b + trio[(m + step) % 3], n))
            for b in range(colour, columns, NCOL)
            for m in range(3)
            for n in range(tiles)
        ]
        return hop(value, pairs)

    def beside(value, step):
        return hop(value, [((c, n), (c + step, n)) for c in everywhere for n in range(tiles)])

    def pick(colours, dtype, state):
        return kernel_call(
            functools.partial(pick_kernel, tiles, colours),
            jax.ShapeDtypeStruct((len(colours) * size, members), dtype),
            [state, obs_rows, place],
            "pick",
            2 * size * tile_rows * members * len(colours) * (1 if dtype == BF16 else 3),
            smem=(2,),
        )

    def collected(rows, colour):
        args = [rows, along_gx(rows, colour, 1), along_gx(rows, colour, 2)]
        shape = jax.ShapeDtypeStruct((size, members), BF16)
        return over_gy(kernel_call(copies_kernel, shape, args, "copies", 1_000_000))

    def transform(pieces, variance):
        return kernel_call(
            root_kernel,
            jax.ShapeDtypeStruct((size, members), BF16),
            [pieces, variance],
            "root",
            8_000_000_000,
        )

    def move(parts, count, sources, dtype, name="rows"):
        rows = parts.shape[0] // count
        return kernel_call(
            functools.partial(rows_kernel, count),
            jax.ShapeDtypeStruct((rows, members), dtype),
            [parts, *[ref for pair in sources for ref in pair]],
            name,
            4 * rows * size * members * len(sources),
        )

    together = lax.optimization_barrier
    parts0 = over_gy(pick((0,), BF16, anomalies))
    total0 = kernel_call(
        functools.partial(sum_kernel, tiles),
        jax.ShapeDtypeStruct((share, members), BF16),
        [parts0],
        "sum",
        1_000_000,
    )
    picked = [None, *[pick((colour,), F32, anomalies) for colour in range(1, NCOL)]]

    pairs = [((target,), source) for target in range(1, NCOL) for source in range(target)]
    own_var, _ = together((obs_var, total0))
    prepared = kernel_call(
        functools.partial(setup_kernel, pairs, tiles, tile_rows),
        [jax.ShapeDtypeStruct((len(t) * share, 1), F32) for t, _ in pairs]
        + [jax.ShapeDtypeStruct((1, 1), F32)] * NCOL
        + [jax.ShapeDtypeStruct((1, size), F32)] * NCOL,
        [obs_rows, levels, place, obs_var, beside(own_var, 1), beside(own_var, -1)],
        "setup",
        1_000_000,
        smem=(1, 2),
    )
    row_factor = {(t[0], source): out for (t, source), out in zip(pairs, prepared)}
    tile_factor = prepared[len(pairs) : len(pairs) + NCOL]
    variance = prepared[len(pairs) + NCOL :]

    state = anomalies
    rows = total0
    done = []
    for colour in range(NCOL):
        pieces = collected(rows, colour)
        if colour < NCOL - 1:
            coming, pieces = together((picked[colour + 1], pieces))
            parts = over_gy(coming)
        var, state = together((variance[colour], state))
        done.append(transform(pieces, var))
        state_factor = [(done[colour], tile_factor[colour])]
        if colour < NCOL - 1:
            sources = [(done[n], row_factor[colour + 1, n]) for n in range(colour + 1)]
            rows = move(parts, tiles, sources, BF16)
        state = move(state, 1, state_factor, F32, "tile")
    return state


def solution(mesh):
    in_specs = (P(AXES, None), P(), P("gx", None), P())
    return jax.shard_map(
        on_device,
        mesh=mesh,
        in_specs=in_specs,
        out_specs=P(AXES, None),
        check_vma=False,
    )
```

```python
import functools

import jax
import jax.numpy as jnp
from jax import lax
from jax.experimental import pallas as pl
from jax.experimental.pallas import tpu as pltpu
from jax.sharding import PartitionSpec as P

NCOL = 4
NS_STEPS = 12
AXES = ("gx", "gy")
VMEM_LIMIT = 20 << 20
INTERPRET = False
F32 = jnp.float32
BF16 = jnp.bfloat16


def kernel_call(body, out, args, name, flops, smem=(), scratch=()):
    whole = pl.BlockSpec(memory_space=pltpu.VMEM)
    scalar = pl.BlockSpec(memory_space=pltpu.SMEM)
    leaves = [*args, *jax.tree.leaves(out)]
    return pl.pallas_call(
        body,
        out_shape=out,
        in_specs=[scalar if n in smem else whole for n in range(len(args))],
        out_specs=jax.tree.map(lambda _: whole, out),
        scratch_shapes=scratch,
        name=name,
        interpret=INTERPRET,
        cost_estimate=pl.CostEstimate(
            flops=flops,
            bytes_accessed=sum(leaf.size * leaf.dtype.itemsize for leaf in leaves),
            transcendentals=0,
        ),
        compiler_params=pltpu.CompilerParams(vmem_limit_bytes=VMEM_LIMIT),
    )(*args)


def dot(left, right):
    return jnp.dot(left, right, preferred_element_type=F32)


def dot_nt(left, right):
    return lax.dot_general(
        left, right, (((1,), (1,)), ((), ())), preferred_element_type=F32
    )


def halves(value):
    high = value.astype(BF16)
    return high, (value - high.astype(F32)).astype(BF16)


def mat_prod(left, right):
    return dot(left[0], right[0]) + (dot(left[0], right[1]) + dot(left[1], right[0]))


def standing(col, colour, columns):
    offset = lax.rem(col + (NCOL - colour), NCOL)
    slot = jnp.where(offset == 1, 2, jnp.where(offset == 3, 0, 1))
    return slot, offset != 2, lax.rem(col - slot + 1 + columns, columns)


def pick_kernel(colours, state, obs, place, *refs):
    outs, scratch = refs[:-1], refs[-1]
    tiles = len(outs)
    tile_rows = state.shape[0]
    columns, size = obs.shape
    share = size // tiles
    col, tile = place[0, 0], place[0, 1]
    band = state.shape[1] // tiles
    for n, colour in enumerate(colours):
        slot, active, batch = standing(col, colour, columns)
        first = jnp.where(active, (slot * tiles + tile) * tile_rows, -(1 << 20))
        local = obs[pl.ds(batch, 1), :] - first
        spots = lax.broadcasted_iota(jnp.int32, (tile_rows, size), 0)
        chosen = jnp.where(spots == local, 1.0, 0.0).T.astype(BF16)

        def pick_band(m, _):
            lanes = pl.ds(pl.multiple_of(m * band, band), band)
            rest = state[:, lanes]
            high = rest.astype(BF16)
            picked = dot(chosen, high)
            if scratch.dtype == F32:
                rest = rest - high.astype(F32)
                middle = rest.astype(BF16)
                picked = picked + dot(chosen, middle)
                picked = picked + dot(chosen, (rest - middle.astype(F32)).astype(BF16))
            scratch[:, lanes] = picked.astype(scratch.dtype)
            return 0

        lax.fori_loop(0, tiles, pick_band, 0)
        for step, out in enumerate(outs):
            start = pl.multiple_of(lax.rem(tile + step, tiles) * share, share)
            out[n * share : (n + 1) * share, :] = scratch[pl.ds(start, share), :]


def setup_kernel(pairs, tiles, tile_rows, obs, levels, place, own, left, right, *outs):
    columns, size = obs.shape
    share = size // tiles
    col, tile = place[0, 0], place[0, 1]
    members = place[0, 2].astype(F32)
    lane = lax.broadcasted_iota(jnp.int32, (share, size), 1)
    mine = lane == lax.broadcasted_iota(jnp.int32, (share, size), 0) + tile * share

    def factor(source, which):
        slot, active, batch = standing(col, source, columns)
        level = levels[batch, slot * tiles + which].astype(F32) / 3.0
        return jnp.where(active, level, 0.0)

    for (targets, source), out in zip(pairs, outs):
        for n, target in enumerate(targets):
            slot, _, batch = standing(col, target, columns)
            inside = obs[pl.ds(batch, 1), :] - slot * (tiles * tile_rows)
            row = jnp.zeros((1, size), F32)
            for which in range(tiles):
                hit = (inside >= which * tile_rows) & (inside < (which + 1) * tile_rows)
                row = jnp.where(hit, factor(source, which), row)
            column = jnp.sum(jnp.where(mine, row, 0.0), axis=1, keepdims=True)
            out[n * share : (n + 1) * share, :] = column / members
    for colour in range(NCOL):
        outs[len(pairs) + colour][...] = jnp.full((1, 1), factor(colour, tile)) / members
        slot, active, _ = standing(col, colour, columns)
        value = jnp.where(
            active & (slot == 2), left[...], jnp.where(active & (slot == 0), right[...], own[...])
        )
        pieces = [value[:, n * share : (n + 1) * share] for n in range(tiles)]
        ordered = []
        for step in range(tiles):
            source = lax.rem(tile + tiles - step, tiles)
            piece = pieces[0]
            for n in range(1, tiles):
                piece = jnp.where(source == n, pieces[n], piece)
            ordered.append(piece)
        outs[len(pairs) + NCOL + colour][...] = jnp.concatenate(ordered, axis=1)


def root_kernel(*refs):
    *pieces, variance, out = refs
    observed = jnp.concatenate([piece[...] for piece in pieces], axis=0)
    size, members = observed.shape
    row = lax.broadcasted_iota(jnp.int32, (size, size), 0)
    column = lax.broadcasted_iota(jnp.int32, (size, size), 1)
    eye = jnp.where(row == column, 1.0, 0.0).astype(F32)
    gram = dot_nt(observed, observed) / (members - 1) + eye * variance[...]
    trace = jnp.sum(jnp.sum(gram * eye, axis=1, keepdims=True), axis=0, keepdims=True)
    left = gram / trace
    right_h = halves(1.5 * eye - 0.5 * left)
    left_h = halves(mat_prod(halves(left), right_h))

    def next_term(left_h, right_h):
        return halves(1.5 * eye - 0.5 * mat_prod(right_h, left_h))

    def step(_, pair):
        left_h, right_h = pair
        term_h = next_term(left_h, right_h)
        return halves(mat_prod(left_h, term_h)), halves(mat_prod(term_h, right_h))

    left_h, right_h = lax.fori_loop(1, NS_STEPS - 1, step, (left_h, right_h))
    right = mat_prod(next_term(left_h, right_h), right_h)
    inverse_half = (right / jnp.sqrt(trace)).astype(BF16)
    out[...] = dot(inverse_half, observed).astype(BF16)


def summed(parts):
    total = parts[0][...]
    for part in parts[1:]:
        total = total + part[...]
    return total


def rows_kernel(count, which, *refs):
    *pairs, out = refs[count:]
    share = out.shape[0]
    rows = summed([ref.at[which * share : (which + 1) * share, :] for ref in refs[:count]])
    for transformed, factor in zip(pairs[::2], pairs[1::2]):
        source = transformed[...]
        projected = dot_nt(rows.astype(BF16), source).astype(BF16)
        rows = rows - factor[...] * dot(projected, source)
    out[...] = rows.astype(out.dtype)


def tile_kernel(state, transformed, factor, out):
    value = state[...]
    source = transformed[...]
    projected = dot_nt(value.astype(BF16), source).astype(BF16)
    out[...] = value - factor[...] * dot(projected, source)


def sum_kernel(*refs):
    *parts, out = refs
    out[...] = summed(parts)


def on_device(anomalies, obs_rows, obs_var, taper_level):
    tile_rows, members = anomalies.shape
    batches, size = obs_rows.shape
    columns = lax.axis_size("gx")
    tiles = lax.axis_size("gy")
    share = size // tiles
    col = lax.axis_index("gx")
    tile = lax.axis_index("gy")
    place = jnp.stack([col, tile, jnp.int32(members - 1)]).astype(jnp.int32).reshape(1, 3)
    levels = taper_level.reshape(batches, 3 * tiles)
    everywhere = list(range(columns))

    def hop(value, pairs):
        flat = [
            ((a % columns) * tiles + b % tiles, (c % columns) * tiles + d % tiles)
            for (a, b), (c, d) in pairs
        ]
        return lax.ppermute(value, AXES, flat)

    def along_gy(value, step):
        return hop(value, [((c, n), (c, n + step)) for c in everywhere for n in range(tiles)])

    def along_gx(value, colour, step):
        trio = (-1, 0, 1)
        pairs = [
            ((b + trio[m], n), (b + trio[(m + step) % 3], n))
            for b in range(colour, columns, NCOL)
            for m in range(3)
            for n in range(tiles)
        ]
        pairs += [
            ((b + 2, n), (b + 2, n + 1 - 2 * (n % 2)))
            for b in range(colour, columns, NCOL)
            for n in range(tiles)
        ]
        return hop(value, pairs)

    def beside(value, step):
        return hop(value, [((c, n), (c + step, n)) for c in everywhere for n in range(tiles)])

    def pick(colours, dtype, state):
        shape = jax.ShapeDtypeStruct((len(colours) * share, members), dtype)
        return kernel_call(
            functools.partial(pick_kernel, colours),
            [shape] * tiles,
            [state, obs_rows, place],
            "pick",
            2 * size * tile_rows * members * len(colours) * (1 if dtype == BF16 else 3),
            smem=(2,),
            scratch=[pltpu.VMEM((size, members), dtype)],
        )

    def scattered(parts):
        return [parts[0], *[along_gy(parts[n], n) for n in range(1, tiles)]]

    def added(parts):
        shape = jax.ShapeDtypeStruct(parts[0].shape, parts[0].dtype)
        return kernel_call(sum_kernel, shape, parts, "sum", 1_000_000)

    def collected(rows, colour):
        first, second = (along_gx(rows, colour, step) for step in (1, 2))
        whole = added([rows, first, second])
        return [whole, *[along_gy(whole, step) for step in range(1, tiles)]]

    def transform(pieces, variance):
        return kernel_call(
            root_kernel,
            jax.ShapeDtypeStruct((size, members), BF16),
            [*pieces, variance],
            "root",
            1_000_000,
        )

    def move_tile(state, transformed, factor):
        return kernel_call(
            tile_kernel,
            jax.ShapeDtypeStruct(state.shape, F32),
            [state, transformed, factor],
            "tile",
            4 * tile_rows * size * members,
        )

    def move(parts, which, sources, dtype):
        rows = share
        return kernel_call(
            functools.partial(rows_kernel, len(parts), which),
            jax.ShapeDtypeStruct((rows, members), dtype),
            [*parts, *[ref for pair in sources for ref in pair]],
            "rows",
            4 * rows * size * members * len(sources),
        )

    together = lax.optimization_barrier
    total0 = added(scattered(pick((0,), BF16, anomalies)))
    later, total0 = together((pick(range(1, NCOL), F32, anomalies), total0))
    parts = scattered(later)

    pairs = [((target,), source) for target in range(1, NCOL) for source in range(target)]
    prepared = kernel_call(
        functools.partial(setup_kernel, pairs, tiles, tile_rows),
        [jax.ShapeDtypeStruct((len(t) * share, 1), F32) for t, _ in pairs]
        + [jax.ShapeDtypeStruct((1, 1), F32)] * NCOL
        + [jax.ShapeDtypeStruct((1, size), F32)] * NCOL,
        [obs_rows, levels, place, obs_var, beside(obs_var, 1), beside(obs_var, -1)],
        "setup",
        1_000_000,
        smem=(1, 2),
    )
    row_factor = {(t[0], source): out for (t, source), out in zip(pairs, prepared)}
    tile_factor = prepared[len(pairs) : len(pairs) + NCOL]
    variance = prepared[len(pairs) + NCOL :]

    state = anomalies
    rows = total0
    done = []
    for colour in range(NCOL):
        pieces = collected(rows, colour)
        var, state = together((variance[colour], state))
        done.append(transform(pieces, var))
        if colour < NCOL - 1:
            sources = [(done[n], row_factor[colour + 1, n]) for n in range(colour + 1)]
            rows = move(parts, colour, sources, BF16)
        state = move_tile(state, done[colour], tile_factor[colour])
    return state


def solution(mesh):
    in_specs = (P(AXES, None), P(), P("gx", None), P())
    return jax.shard_map(
        on_device,
        mesh=mesh,
        in_specs=in_specs,
        out_specs=P(AXES, None),
        check_vma=False,
    )
```

```python
import functools

import jax
import jax.numpy as jnp
from jax import lax
from jax.experimental import pallas as pl
from jax.experimental.pallas import tpu as pltpu
from jax.sharding import PartitionSpec as P

NCOL = 4
NS_STEPS = 12
AXES = ("gx", "gy")
VMEM_LIMIT = 20 << 20
INTERPRET = False
F32 = jnp.float32
BF16 = jnp.bfloat16


def kernel_call(body, out, args, name, flops, smem=(), scratch=()):
    whole = pl.BlockSpec(memory_space=pltpu.VMEM)
    scalar = pl.BlockSpec(memory_space=pltpu.SMEM)
    leaves = [*args, *jax.tree.leaves(out)]
    return pl.pallas_call(
        body,
        out_shape=out,
        in_specs=[scalar if n in smem else whole for n in range(len(args))],
        out_specs=jax.tree.map(lambda _: whole, out),
        scratch_shapes=scratch,
        name=name,
        interpret=INTERPRET,
        cost_estimate=pl.CostEstimate(
            flops=flops,
            bytes_accessed=sum(leaf.size * leaf.dtype.itemsize for leaf in leaves),
            transcendentals=0,
        ),
        compiler_params=pltpu.CompilerParams(vmem_limit_bytes=VMEM_LIMIT),
    )(*args)


def dot(left, right):
    return jnp.dot(left, right, preferred_element_type=F32)


def dot_nt(left, right):
    return lax.dot_general(
        left, right, (((1,), (1,)), ((), ())), preferred_element_type=F32
    )


def halves(value):
    high = value.astype(BF16)
    return high, (value - high.astype(F32)).astype(BF16)


def mat_prod(left, right):
    return dot(left[0], right[0]) + (dot(left[0], right[1]) + dot(left[1], right[0]))


def standing(col, colour, columns):
    offset = lax.rem(col + (NCOL - colour), NCOL)
    slot = jnp.where(offset == 1, 2, jnp.where(offset == 3, 0, 1))
    return slot, offset != 2, lax.rem(col - slot + 1 + columns, columns)


def pick_kernel(colours, state, obs, place, *refs):
    outs, scratch = refs[:-1], refs[-1]
    tiles = len(outs)
    tile_rows = state.shape[0]
    columns, size = obs.shape
    share = size // tiles
    col, tile = place[0, 0], place[0, 1]
    band = state.shape[1] // tiles
    for n, colour in enumerate(colours):
        slot, active, batch = standing(col, colour, columns)
        first = jnp.where(active, (slot * tiles + tile) * tile_rows, -(1 << 20))
        local = obs[pl.ds(batch, 1), :] - first
        spots = lax.broadcasted_iota(jnp.int32, (tile_rows, size), 0)
        chosen = jnp.where(spots == local, 1.0, 0.0).T.astype(BF16)

        def pick_band(m, _):
            lanes = pl.ds(pl.multiple_of(m * band, band), band)
            rest = state[:, lanes]
            high = rest.astype(BF16)
            picked = dot(chosen, high)
            if scratch.dtype == F32:
                rest = rest - high.astype(F32)
                middle = rest.astype(BF16)
                picked = picked + dot(chosen, middle)
                picked = picked + dot(chosen, (rest - middle.astype(F32)).astype(BF16))
            scratch[:, lanes] = picked.astype(scratch.dtype)
            return 0

        lax.fori_loop(0, tiles, pick_band, 0)
        for step, out in enumerate(outs):
            start = pl.multiple_of(lax.rem(tile + step, tiles) * share, share)
            out[n * share : (n + 1) * share, :] = scratch[pl.ds(start, share), :]


def setup_kernel(pairs, tiles, tile_rows, obs, levels, place, own, left, right, *outs):
    columns, size = obs.shape
    share = size // tiles
    col, tile = place[0, 0], place[0, 1]
    members = place[0, 2].astype(F32)
    lane = lax.broadcasted_iota(jnp.int32, (share, size), 1)
    mine = lane == lax.broadcasted_iota(jnp.int32, (share, size), 0) + tile * share

    def factor(source, which):
        slot, active, batch = standing(col, source, columns)
        level = levels[batch, slot * tiles + which].astype(F32) / 3.0
        return jnp.where(active, level, 0.0)

    for (targets, source), out in zip(pairs, outs):
        for n, target in enumerate(targets):
            slot, _, batch = standing(col, target, columns)
            inside = obs[pl.ds(batch, 1), :] - slot * (tiles * tile_rows)
            row = jnp.zeros((1, size), F32)
            for which in range(tiles):
                hit = (inside >= which * tile_rows) & (inside < (which + 1) * tile_rows)
                row = jnp.where(hit, factor(source, which), row)
            column = jnp.sum(jnp.where(mine, row, 0.0), axis=1, keepdims=True)
            out[n * share : (n + 1) * share, :] = column / members
    for colour in range(NCOL):
        outs[len(pairs) + colour][...] = jnp.full((1, 1), factor(colour, tile)) / members
        slot, active, _ = standing(col, colour, columns)
        value = jnp.where(
            active & (slot == 2), left[...], jnp.where(active & (slot == 0), right[...], own[...])
        )
        pieces = [value[:, n * share : (n + 1) * share] for n in range(tiles)]
        ordered = []
        for step in range(tiles):
            source = lax.rem(tile + tiles - step, tiles)
            piece = pieces[0]
            for n in range(1, tiles):
                piece = jnp.where(source == n, pieces[n], piece)
            ordered.append(piece)
        outs[len(pairs) + NCOL + colour][...] = jnp.concatenate(ordered, axis=1)


def root_kernel(*refs):
    *pieces, variance, out = refs
    observed = jnp.concatenate([piece[...] for piece in pieces], axis=0)
    size, members = observed.shape
    row = lax.broadcasted_iota(jnp.int32, (size, size), 0)
    column = lax.broadcasted_iota(jnp.int32, (size, size), 1)
    eye = jnp.where(row == column, 1.0, 0.0).astype(F32)
    gram = dot_nt(observed, observed) / (members - 1) + eye * variance[...]
    trace = jnp.sum(jnp.sum(gram * eye, axis=1, keepdims=True), axis=0, keepdims=True)
    left = gram / trace
    right_h = halves(1.5 * eye - 0.5 * left)
    left_h = halves(mat_prod(halves(left), right_h))

    def next_term(left_h, right_h):
        return halves(1.5 * eye - 0.5 * mat_prod(right_h, left_h))

    def step(_, pair):
        left_h, right_h = pair
        term_h = next_term(left_h, right_h)
        return halves(mat_prod(left_h, term_h)), halves(mat_prod(term_h, right_h))

    left_h, right_h = lax.fori_loop(1, NS_STEPS - 1, step, (left_h, right_h))
    right = mat_prod(next_term(left_h, right_h), right_h)
    inverse_half = (right / jnp.sqrt(trace)).astype(BF16)
    out[...] = dot(inverse_half, observed).astype(BF16)


def summed(parts):
    total = parts[0][...]
    for part in parts[1:]:
        total = total + part[...]
    return total


def rows_kernel(count, *refs):
    *pairs, out = refs[count:]
    rows = summed(refs[:count])
    for transformed, factor in zip(pairs[::2], pairs[1::2]):
        source = transformed[...]
        projected = dot_nt(rows.astype(BF16), source).astype(BF16)
        rows = rows - factor[...] * dot(projected, source)
    out[...] = rows.astype(out.dtype)


def tile_kernel(state, transformed, factor, out):
    value = state[...]
    source = transformed[...]
    projected = dot_nt(value.astype(BF16), source).astype(BF16)
    out[...] = value - factor[...] * dot(projected, source)


def sum_kernel(*refs):
    *parts, out = refs
    out[...] = summed(parts)


def on_device(anomalies, obs_rows, obs_var, taper_level):
    tile_rows, members = anomalies.shape
    batches, size = obs_rows.shape
    columns = lax.axis_size("gx")
    tiles = lax.axis_size("gy")
    share = size // tiles
    col = lax.axis_index("gx")
    tile = lax.axis_index("gy")
    place = jnp.stack([col, tile, jnp.int32(members - 1)]).astype(jnp.int32).reshape(1, 3)
    levels = taper_level.reshape(batches, 3 * tiles)
    everywhere = list(range(columns))

    def hop(value, pairs):
        flat = [
            ((a % columns) * tiles + b % tiles, (c % columns) * tiles + d % tiles)
            for (a, b), (c, d) in pairs
        ]
        return lax.ppermute(value, AXES, flat)

    def along_gy(value, step):
        return hop(value, [((c, n), (c, n + step)) for c in everywhere for n in range(tiles)])

    def along_gx(value, colour, step):
        trio = (-1, 0, 1)
        pairs = [
            ((b + trio[m], n), (b + trio[(m + step) % 3], n))
            for b in range(colour, columns, NCOL)
            for m in range(3)
            for n in range(tiles)
        ]
        pairs += [
            ((b + 2, n), (b + 2, n + 1 - 2 * (n % 2)))
            for b in range(colour, columns, NCOL)
            for n in range(tiles)
        ]
        return hop(value, pairs)

    def beside(value, step):
        return hop(value, [((c, n), (c + step, n)) for c in everywhere for n in range(tiles)])

    def pick(colours, dtype, state):
        shape = jax.ShapeDtypeStruct((len(colours) * share, members), dtype)
        return kernel_call(
            functools.partial(pick_kernel, colours),
            [shape] * tiles,
            [state, obs_rows, place],
            "pick",
            2 * size * tile_rows * members * len(colours) * (1 if dtype == BF16 else 3),
            smem=(2,),
            scratch=[pltpu.VMEM((size, members), dtype)],
        )

    def scattered(parts):
        return [parts[0], *[along_gy(parts[n], n) for n in range(1, tiles)]]

    def added(parts):
        shape = jax.ShapeDtypeStruct(parts[0].shape, parts[0].dtype)
        return kernel_call(sum_kernel, shape, parts, "sum", 1_000_000)

    def joined(rows, colour):
        first, second = (along_gx(rows, colour, step) for step in (1, 2))
        return added([rows, first, second])

    def spread(whole):
        return [whole, *[along_gy(whole, step) for step in range(1, tiles)]]

    def transform(pieces, variance):
        return kernel_call(
            root_kernel,
            jax.ShapeDtypeStruct((size, members), BF16),
            [*pieces, variance],
            "root",
            8_000_000_000,
        )

    def move_tile(state, transformed, factor):
        return kernel_call(
            tile_kernel,
            jax.ShapeDtypeStruct(state.shape, F32),
            [state, transformed, factor],
            "tile",
            4 * tile_rows * size * members,
        )

    def move(parts, sources, dtype):
        rows = share
        return kernel_call(
            functools.partial(rows_kernel, len(parts)),
            jax.ShapeDtypeStruct((rows, members), dtype),
            [*parts, *[ref for pair in sources for ref in pair]],
            "rows",
            4 * rows * size * members * len(sources),
        )

    together = lax.optimization_barrier
    total0 = added(scattered(pick((0,), BF16, anomalies)))
    picked = [None, *[pick((colour,), F32, anomalies) for colour in range(1, NCOL)]]

    pairs = [((target,), source) for target in range(1, NCOL) for source in range(target)]
    prepared = kernel_call(
        functools.partial(setup_kernel, pairs, tiles, tile_rows),
        [jax.ShapeDtypeStruct((len(t) * share, 1), F32) for t, _ in pairs]
        + [jax.ShapeDtypeStruct((1, 1), F32)] * NCOL
        + [jax.ShapeDtypeStruct((1, size), F32)] * NCOL,
        [obs_rows, levels, place, obs_var, beside(obs_var, 1), beside(obs_var, -1)],
        "setup",
        1_000_000,
        smem=(1, 2),
    )
    row_factor = {(t[0], source): out for (t, source), out in zip(pairs, prepared)}
    tile_factor = prepared[len(pairs) : len(pairs) + NCOL]
    variance = prepared[len(pairs) + NCOL :]

    state = anomalies
    rows = total0
    done = []
    for colour in range(NCOL):
        whole = joined(rows, colour)
        pieces = spread(whole)
        if colour < NCOL - 1:
            coming, _ = together((picked[colour + 1], whole))
            parts = scattered(coming)
        var, state = together((variance[colour], state))
        done.append(transform(pieces, var))
        if colour < NCOL - 1:
            sources = [(done[n], row_factor[colour + 1, n]) for n in range(colour + 1)]
            rows = move(parts, sources, BF16)
        state = move_tile(state, done[colour], tile_factor[colour])
    return state


def solution(mesh):
    in_specs = (P(AXES, None), P(), P("gx", None), P())
    return jax.shard_map(
        on_device,
        mesh=mesh,
        in_specs=in_specs,
        out_specs=P(AXES, None),
        check_vma=False,
    )
```

```python
import functools

import jax
import jax.numpy as jnp
from jax import lax
from jax.experimental import pallas as pl
from jax.experimental.pallas import tpu as pltpu
from jax.sharding import PartitionSpec as P

NCOL = 4
NS_STEPS = 12
AXES = ("gx", "gy")
VMEM_LIMIT = 20 << 20
INTERPRET = False
F32 = jnp.float32
BF16 = jnp.bfloat16


def kernel_call(body, out, args, name, flops, smem=(), scratch=()):
    whole = pl.BlockSpec(memory_space=pltpu.VMEM)
    scalar = pl.BlockSpec(memory_space=pltpu.SMEM)
    leaves = [*args, *jax.tree.leaves(out)]
    return pl.pallas_call(
        body,
        out_shape=out,
        in_specs=[scalar if n in smem else whole for n in range(len(args))],
        out_specs=jax.tree.map(lambda _: whole, out),
        scratch_shapes=scratch,
        name=name,
        interpret=INTERPRET,
        cost_estimate=pl.CostEstimate(
            flops=flops,
            bytes_accessed=sum(leaf.size * leaf.dtype.itemsize for leaf in leaves),
            transcendentals=0,
        ),
        compiler_params=pltpu.CompilerParams(vmem_limit_bytes=VMEM_LIMIT),
    )(*args)


def dot(left, right):
    return jnp.dot(left, right, preferred_element_type=F32)


def dot_nt(left, right):
    return lax.dot_general(
        left, right, (((1,), (1,)), ((), ())), preferred_element_type=F32
    )


def halves(value):
    high = value.astype(BF16)
    return high, (value - high.astype(F32)).astype(BF16)


def mat_prod(left, right):
    return dot(left[0], right[0]) + (dot(left[0], right[1]) + dot(left[1], right[0]))


def standing(col, colour, columns):
    offset = lax.rem(col + (NCOL - colour), NCOL)
    slot = jnp.where(offset == 1, 2, jnp.where(offset == 3, 0, 1))
    return slot, offset != 2, lax.rem(col - slot + 1 + columns, columns)


def pick_kernel(colours, state, obs, place, *refs):
    outs, scratch = refs[:-1], refs[-1]
    tiles = len(outs)
    tile_rows = state.shape[0]
    columns, size = obs.shape
    share = size // tiles
    col, tile = place[0, 0], place[0, 1]
    band = state.shape[1] // tiles
    for n, colour in enumerate(colours):
        slot, active, batch = standing(col, colour, columns)
        first = jnp.where(active, (slot * tiles + tile) * tile_rows, -(1 << 20))
        local = obs[pl.ds(batch, 1), :] - first
        row = lax.broadcasted_iota(jnp.int32, (size, size), 0)
        same = row == lax.broadcasted_iota(jnp.int32, (size, size), 1)
        wanted = jnp.sum(jnp.where(same, local.astype(F32), 0.0), axis=1, keepdims=True)
        spots = lax.broadcasted_iota(jnp.int32, (size, tile_rows), 1)
        chosen = jnp.where(spots == wanted.astype(jnp.int32), 1.0, 0.0).astype(BF16)

        def pick_band(m, _):
            lanes = pl.ds(pl.multiple_of(m * band, band), band)
            rest = state[:, lanes]
            high = rest.astype(BF16)
            picked = dot(chosen, high)
            if scratch.dtype == F32:
                rest = rest - high.astype(F32)
                middle = rest.astype(BF16)
                picked = picked + dot(chosen, middle)
                picked = picked + dot(chosen, (rest - middle.astype(F32)).astype(BF16))
            scratch[:, lanes] = picked.astype(scratch.dtype)
            return 0

        lax.fori_loop(0, tiles, pick_band, 0)
        for step, out in enumerate(outs):
            start = pl.multiple_of(lax.rem(tile + step, tiles) * share, share)
            out[n * share : (n + 1) * share, :] = scratch[pl.ds(start, share), :]


def setup_kernel(pairs, tiles, tile_rows, obs, levels, place, own, left, right, *outs):
    columns, size = obs.shape
    share = size // tiles
    col, tile = place[0, 0], place[0, 1]
    members = place[0, 2].astype(F32)
    lane = lax.broadcasted_iota(jnp.int32, (share, size), 1)
    mine = lane == lax.broadcasted_iota(jnp.int32, (share, size), 0) + tile * share

    def factor(source, which):
        slot, active, batch = standing(col, source, columns)
        level = levels[batch, slot * tiles + which].astype(F32) / 3.0
        return jnp.where(active, level, 0.0)

    for (targets, source), out in zip(pairs, outs):
        for n, target in enumerate(targets):
            slot, _, batch = standing(col, target, columns)
            inside = obs[pl.ds(batch, 1), :] - slot * (tiles * tile_rows)
            row = jnp.zeros((1, size), F32)
            for which in range(tiles):
                hit = (inside >= which * tile_rows) & (inside < (which + 1) * tile_rows)
                row = jnp.where(hit, factor(source, which), row)
            column = jnp.sum(jnp.where(mine, row, 0.0), axis=1, keepdims=True)
            out[n * share : (n + 1) * share, :] = column / members
    for colour in range(NCOL):
        outs[len(pairs) + colour][...] = jnp.full((1, 1), factor(colour, tile)) / members
        slot, active, _ = standing(col, colour, columns)
        value = jnp.where(
            active & (slot == 2), left[...], jnp.where(active & (slot == 0), right[...], own[...])
        )
        pieces = [value[:, n * share : (n + 1) * share] for n in range(tiles)]
        ordered = []
        for step in range(tiles):
            source = lax.rem(tile + tiles - step, tiles)
            piece = pieces[0]
            for n in range(1, tiles):
                piece = jnp.where(source == n, pieces[n], piece)
            ordered.append(piece)
        outs[len(pairs) + NCOL + colour][...] = jnp.concatenate(ordered, axis=1)


def root_kernel(*refs):
    *pieces, variance, out = refs
    observed = jnp.concatenate([piece[...] for piece in pieces], axis=0)
    size, members = observed.shape
    row = lax.broadcasted_iota(jnp.int32, (size, size), 0)
    column = lax.broadcasted_iota(jnp.int32, (size, size), 1)
    eye = jnp.where(row == column, 1.0, 0.0).astype(F32)
    gram = dot_nt(observed, observed) / (members - 1) + eye * variance[...]
    trace = jnp.sum(jnp.sum(gram * eye, axis=1, keepdims=True), axis=0, keepdims=True)
    left = gram / trace
    right_h = halves(1.5 * eye - 0.5 * left)
    left_h = halves(mat_prod(halves(left), right_h))

    def next_term(left_h, right_h):
        return halves(1.5 * eye - 0.5 * mat_prod(right_h, left_h))

    def step(_, pair):
        left_h, right_h = pair
        term_h = next_term(left_h, right_h)
        return halves(mat_prod(left_h, term_h)), halves(mat_prod(term_h, right_h))

    left_h, right_h = lax.fori_loop(1, NS_STEPS - 1, step, (left_h, right_h))
    right = mat_prod(next_term(left_h, right_h), right_h)
    inverse_half = (right / jnp.sqrt(trace)).astype(BF16)
    out[...] = dot(inverse_half, observed).astype(BF16)


def summed(parts):
    total = parts[0][...]
    for part in parts[1:]:
        total = total + part[...]
    return total


def rows_kernel(count, *refs):
    *pairs, out = refs[count:]
    rows = summed(refs[:count])
    for transformed, factor in zip(pairs[::2], pairs[1::2]):
        source = transformed[...]
        projected = dot_nt(rows.astype(BF16), source).astype(BF16)
        rows = rows - factor[...] * dot(projected, source)
    out[...] = rows.astype(out.dtype)


def tile_kernel(state, transformed, factor, out):
    value = state[...]
    source = transformed[...]
    projected = dot_nt(value.astype(BF16), source).astype(BF16)
    out[...] = value - factor[...] * dot(projected, source)


def sum_kernel(*refs):
    *parts, out = refs
    out[...] = summed(parts)


def on_device(anomalies, obs_rows, obs_var, taper_level):
    tile_rows, members = anomalies.shape
    batches, size = obs_rows.shape
    columns = lax.axis_size("gx")
    tiles = lax.axis_size("gy")
    share = size // tiles
    col = lax.axis_index("gx")
    tile = lax.axis_index("gy")
    place = jnp.stack([col, tile, jnp.int32(members - 1)]).astype(jnp.int32).reshape(1, 3)
    levels = taper_level.reshape(batches, 3 * tiles)
    everywhere = list(range(columns))

    def hop(value, pairs):
        flat = [
            ((a % columns) * tiles + b % tiles, (c % columns) * tiles + d % tiles)
            for (a, b), (c, d) in pairs
        ]
        return lax.ppermute(value, AXES, flat)

    def along_gy(value, step):
        return hop(value, [((c, n), (c, n + step)) for c in everywhere for n in range(tiles)])

    def along_gx(value, colour, step):
        trio = (-1, 0, 1)
        pairs = [
            ((b + trio[m], n), (b + trio[(m + step) % 3], n))
            for b in range(colour, columns, NCOL)
            for m in range(3)
            for n in range(tiles)
        ]
        pairs += [
            ((b + 2, n), (b + 2, n + 1 - 2 * (n % 2)))
            for b in range(colour, columns, NCOL)
            for n in range(tiles)
        ]
        return hop(value, pairs)

    def beside(value, step):
        return hop(value, [((c, n), (c + step, n)) for c in everywhere for n in range(tiles)])

    def pick(colours, dtype, state):
        shape = jax.ShapeDtypeStruct((len(colours) * share, members), dtype)
        return kernel_call(
            functools.partial(pick_kernel, colours),
            [shape] * tiles,
            [state, obs_rows, place],
            "pick",
            2 * size * tile_rows * members * len(colours) * (1 if dtype == BF16 else 3),
            smem=(2,),
            scratch=[pltpu.VMEM((size, members), dtype)],
        )

    def scattered(parts):
        return [parts[0], *[along_gy(parts[n], n) for n in range(1, tiles)]]

    def added(parts):
        shape = jax.ShapeDtypeStruct(parts[0].shape, parts[0].dtype)
        return kernel_call(sum_kernel, shape, parts, "sum", 1_000_000)

    def joined(rows, colour):
        first, second = (along_gx(rows, colour, step) for step in (1, 2))
        return added([rows, first, second])

    def spread(whole):
        return [whole, *[along_gy(whole, step) for step in range(1, tiles)]]

    def transform(pieces, variance):
        return kernel_call(
            root_kernel,
            jax.ShapeDtypeStruct((size, members), BF16),
            [*pieces, variance],
            "root",
            8_000_000_000,
        )

    def move_tile(state, transformed, factor):
        blocks = 4
        some = pl.BlockSpec((tile_rows // blocks, members), lambda n: (n, 0))
        return pl.pallas_call(
            tile_kernel,
            out_shape=jax.ShapeDtypeStruct(state.shape, F32),
            grid=(blocks,),
            in_specs=[
                some,
                pl.BlockSpec((size, members), lambda n: (0, 0)),
                pl.BlockSpec((1, 1), lambda n: (0, 0)),
            ],
            out_specs=some,
            name="tile",
            interpret=INTERPRET,
            cost_estimate=pl.CostEstimate(
                flops=4 * tile_rows * size * members,
                bytes_accessed=2 * state.size * 4,
                transcendentals=0,
            ),
            compiler_params=pltpu.CompilerParams(vmem_limit_bytes=VMEM_LIMIT),
        )(state, transformed, factor)

    def move(parts, sources, dtype):
        rows = share
        return kernel_call(
            functools.partial(rows_kernel, len(parts)),
            jax.ShapeDtypeStruct((rows, members), dtype),
            [*parts, *[ref for pair in sources for ref in pair]],
            "rows",
            4 * rows * size * members * len(sources),
        )

    together = lax.optimization_barrier
    total0 = added(scattered(pick((0,), BF16, anomalies)))
    picked = [None, *[pick((colour,), F32, anomalies) for colour in range(1, NCOL)]]

    pairs = [((target,), source) for target in range(1, NCOL) for source in range(target)]
    prepared = kernel_call(
        functools.partial(setup_kernel, pairs, tiles, tile_rows),
        [jax.ShapeDtypeStruct((len(t) * share, 1), F32) for t, _ in pairs]
        + [jax.ShapeDtypeStruct((1, 1), F32)] * NCOL
        + [jax.ShapeDtypeStruct((1, size), F32)] * NCOL,
        [obs_rows, levels, place, obs_var, beside(obs_var, 1), beside(obs_var, -1)],
        "setup",
        1_000_000,
        smem=(1, 2),
    )
    row_factor = {(t[0], source): out for (t, source), out in zip(pairs, prepared)}
    tile_factor = prepared[len(pairs) : len(pairs) + NCOL]
    variance = prepared[len(pairs) + NCOL :]

    state = anomalies
    rows = total0
    done = []
    for colour in range(NCOL):
        whole = joined(rows, colour)
        pieces = spread(whole)
        if colour < NCOL - 1:
            coming, _ = together((picked[colour + 1], whole))
            parts = scattered(coming)
        var, state = together((variance[colour], state))
        done.append(transform(pieces, var))
        if colour < NCOL - 1:
            sources = [(done[n], row_factor[colour + 1, n]) for n in range(colour + 1)]
            rows = move(parts, sources, BF16)
        state = move_tile(state, done[colour], tile_factor[colour])
    return state


def solution(mesh):
    in_specs = (P(AXES, None), P(), P("gx", None), P())
    return jax.shard_map(
        on_device,
        mesh=mesh,
        in_specs=in_specs,
        out_specs=P(AXES, None),
        check_vma=False,
    )
```

```python
import functools

import jax
import jax.numpy as jnp
from jax import lax
from jax.experimental import pallas as pl
from jax.experimental.pallas import tpu as pltpu
from jax.sharding import PartitionSpec as P

NCOL = 4
NS_STEPS = 12
AXES = ("gx", "gy")
VMEM_LIMIT = 20 << 20
INTERPRET = False
F32 = jnp.float32
BF16 = jnp.bfloat16


def kernel_call(body, out, args, name, flops, smem=(), scratch=()):
    whole = pl.BlockSpec(memory_space=pltpu.VMEM)
    scalar = pl.BlockSpec(memory_space=pltpu.SMEM)
    leaves = [*args, *jax.tree.leaves(out)]
    return pl.pallas_call(
        body,
        out_shape=out,
        in_specs=[scalar if n in smem else whole for n in range(len(args))],
        out_specs=jax.tree.map(lambda _: whole, out),
        scratch_shapes=scratch,
        name=name,
        interpret=INTERPRET,
        cost_estimate=pl.CostEstimate(
            flops=flops,
            bytes_accessed=sum(leaf.size * leaf.dtype.itemsize for leaf in leaves),
            transcendentals=0,
        ),
        compiler_params=pltpu.CompilerParams(vmem_limit_bytes=VMEM_LIMIT),
    )(*args)


def dot(left, right):
    return jnp.dot(left, right, preferred_element_type=F32)


def dot_nt(left, right):
    return lax.dot_general(
        left, right, (((1,), (1,)), ((), ())), preferred_element_type=F32
    )


def halves(value):
    high = value.astype(BF16)
    return high, (value - high.astype(F32)).astype(BF16)


def mat_prod(left, right):
    return dot(left[0], right[0]) + (dot(left[0], right[1]) + dot(left[1], right[0]))


def standing(col, colour, columns):
    offset = lax.rem(col + (NCOL - colour), NCOL)
    slot = jnp.where(offset == 1, 2, jnp.where(offset == 3, 0, 1))
    return slot, offset != 2, lax.rem(col - slot + 1 + columns, columns)


def pick_kernel(colours, state, obs, place, *refs):
    outs, scratch = refs[:-1], refs[-1]
    tiles = len(outs)
    tile_rows = state.shape[0]
    columns, size = obs.shape
    share = size // tiles
    col, tile = place[0, 0], place[0, 1]
    band = state.shape[1] // tiles
    for n, colour in enumerate(colours):
        slot, active, batch = standing(col, colour, columns)
        first = jnp.where(active, (slot * tiles + tile) * tile_rows, -(1 << 20))
        local = obs[pl.ds(batch, 1), :] - first
        row = lax.broadcasted_iota(jnp.int32, (size, size), 0)
        same = row == lax.broadcasted_iota(jnp.int32, (size, size), 1)
        wanted = jnp.sum(jnp.where(same, local.astype(F32), 0.0), axis=1, keepdims=True)
        spots = lax.broadcasted_iota(jnp.int32, (size, tile_rows), 1)
        chosen = jnp.where(spots == wanted.astype(jnp.int32), 1.0, 0.0).astype(BF16)

        def pick_band(m, _):
            lanes = pl.ds(pl.multiple_of(m * band, band), band)
            rest = state[:, lanes]
            high = rest.astype(BF16)
            picked = dot(chosen, high)
            if scratch.dtype == F32:
                rest = rest - high.astype(F32)
                middle = rest.astype(BF16)
                picked = picked + dot(chosen, middle)
                picked = picked + dot(chosen, (rest - middle.astype(F32)).astype(BF16))
            scratch[:, lanes] = picked.astype(scratch.dtype)
            return 0

        lax.fori_loop(0, tiles, pick_band, 0)
        for step, out in enumerate(outs):
            start = pl.multiple_of(lax.rem(tile + step, tiles) * share, share)
            out[n * share : (n + 1) * share, :] = scratch[pl.ds(start, share), :]


def setup_kernel(pairs, tiles, tile_rows, obs, levels, place, own, left, right, *outs):
    columns, size = obs.shape
    share = size // tiles
    col, tile = place[0, 0], place[0, 1]
    members = place[0, 2].astype(F32)
    lane = lax.broadcasted_iota(jnp.int32, (share, size), 1)
    mine = lane == lax.broadcasted_iota(jnp.int32, (share, size), 0) + tile * share

    def factor(source, which):
        slot, active, batch = standing(col, source, columns)
        level = levels[batch, slot * tiles + which].astype(F32) / 3.0
        return jnp.where(active, level, 0.0)

    for (targets, source), out in zip(pairs, outs):
        for n, target in enumerate(targets):
            slot, _, batch = standing(col, target, columns)
            inside = obs[pl.ds(batch, 1), :] - slot * (tiles * tile_rows)
            row = jnp.zeros((1, size), F32)
            for which in range(tiles):
                hit = (inside >= which * tile_rows) & (inside < (which + 1) * tile_rows)
                row = jnp.where(hit, factor(source, which), row)
            column = jnp.sum(jnp.where(mine, row, 0.0), axis=1, keepdims=True)
            out[n * share : (n + 1) * share, :] = column / members
    for colour in range(NCOL):
        outs[len(pairs) + colour][...] = jnp.full((1, 1), factor(colour, tile)) / members
        slot, active, _ = standing(col, colour, columns)
        value = jnp.where(
            active & (slot == 2), left[...], jnp.where(active & (slot == 0), right[...], own[...])
        )
        pieces = [value[:, n * share : (n + 1) * share] for n in range(tiles)]
        ordered = []
        for step in range(tiles):
            source = lax.rem(tile + tiles - step, tiles)
            piece = pieces[0]
            for n in range(1, tiles):
                piece = jnp.where(source == n, pieces[n], piece)
            ordered.append(piece)
        outs[len(pairs) + NCOL + colour][...] = jnp.concatenate(ordered, axis=1)


def root_kernel(*refs):
    *pieces, variance, out = refs
    observed = jnp.concatenate([piece[...] for piece in pieces], axis=0)
    size, members = observed.shape
    row = lax.broadcasted_iota(jnp.int32, (size, size), 0)
    column = lax.broadcasted_iota(jnp.int32, (size, size), 1)
    eye = jnp.where(row == column, 1.0, 0.0).astype(F32)
    gram = dot_nt(observed, observed) / (members - 1) + eye * variance[...]
    trace = jnp.sum(jnp.sum(gram * eye, axis=1, keepdims=True), axis=0, keepdims=True)
    left = gram / trace
    right_h = halves(1.5 * eye - 0.5 * left)
    left_h = halves(mat_prod(halves(left), right_h))

    def next_term(left_h, right_h):
        return halves(1.5 * eye - 0.5 * mat_prod(right_h, left_h))

    def step(_, pair):
        left_h, right_h = pair
        term_h = next_term(left_h, right_h)
        return halves(mat_prod(left_h, term_h)), halves(mat_prod(term_h, right_h))

    left_h, right_h = lax.fori_loop(1, NS_STEPS - 1, step, (left_h, right_h))
    right = mat_prod(next_term(left_h, right_h), right_h)
    inverse_half = (right / jnp.sqrt(trace)).astype(BF16)
    out[...] = dot(inverse_half, observed).astype(BF16)


def summed(parts):
    total = parts[0][...]
    for part in parts[1:]:
        total = total + part[...]
    return total


def rows_kernel(count, *refs):
    *pairs, out = refs[count:]
    rows = summed(refs[:count])
    for transformed, factor in zip(pairs[::2], pairs[1::2]):
        source = transformed[...]
        projected = dot_nt(rows.astype(BF16), source).astype(BF16)
        rows = rows - factor[...] * dot(projected, source)
    out[...] = rows.astype(out.dtype)


def tile_kernel(state, transformed, factor, out):
    value = state[...]
    source = transformed[...]
    projected = dot_nt(value.astype(BF16), source).astype(BF16)
    out[...] = value - factor[...] * dot(projected, source)


def sum_kernel(*refs):
    *parts, out = refs
    out[...] = summed(parts)


def on_device(anomalies, obs_rows, obs_var, taper_level):
    tile_rows, members = anomalies.shape
    batches, size = obs_rows.shape
    columns = lax.axis_size("gx")
    tiles = lax.axis_size("gy")
    share = size // tiles
    col = lax.axis_index("gx")
    tile = lax.axis_index("gy")
    place = jnp.stack([col, tile, jnp.int32(members - 1)]).astype(jnp.int32).reshape(1, 3)
    levels = taper_level.reshape(batches, 3 * tiles)
    everywhere = list(range(columns))

    def hop(value, pairs):
        flat = [
            ((a % columns) * tiles + b % tiles, (c % columns) * tiles + d % tiles)
            for (a, b), (c, d) in pairs
        ]
        return lax.ppermute(value, AXES, flat)

    def along_gy(value, step):
        return hop(value, [((c, n), (c, n + step)) for c in everywhere for n in range(tiles)])

    def along_gx(value, colour, step):
        trio = (-1, 0, 1)
        pairs = [
            ((b + trio[m], n), (b + trio[(m + step) % 3], n))
            for b in range(colour, columns, NCOL)
            for m in range(3)
            for n in range(tiles)
        ]
        pairs += [
            ((b + 2, n), (b + 2, n + 1 - 2 * (n % 2)))
            for b in range(colour, columns, NCOL)
            for n in range(tiles)
        ]
        return hop(value, pairs)

    def beside(value, step):
        return hop(value, [((c, n), (c + step, n)) for c in everywhere for n in range(tiles)])

    def pick(colours, dtype, state):
        shape = jax.ShapeDtypeStruct((len(colours) * share, members), dtype)
        return kernel_call(
            functools.partial(pick_kernel, colours),
            [shape] * tiles,
            [state, obs_rows, place],
            "pick",
            2 * size * tile_rows * members * len(colours) * (1 if dtype == BF16 else 3),
            smem=(2,),
            scratch=[pltpu.VMEM((size, members), dtype)],
        )

    def scattered(parts):
        return [parts[0], *[along_gy(parts[n], n) for n in range(1, tiles)]]

    def added(parts):
        shape = jax.ShapeDtypeStruct(parts[0].shape, parts[0].dtype)
        return kernel_call(sum_kernel, shape, parts, "sum", 1_000_000)

    def joined(rows, colour, beside_it):
        first, second = (along_gx(rows, colour, step) for step in (1, 2))
        second, beside_it = lax.optimization_barrier((second, beside_it))
        return added([rows, first, second]), beside_it

    def spread(whole):
        return [whole, *[along_gy(whole, step) for step in range(1, tiles)]]

    def transform(pieces, variance):
        return kernel_call(
            root_kernel,
            jax.ShapeDtypeStruct((size, members), BF16),
            [*pieces, variance],
            "root",
            8_000_000_000,
        )

    def move_tile(state, transformed, factor, blocks):
        some = pl.BlockSpec((tile_rows // blocks, members), lambda n: (n, 0))
        return pl.pallas_call(
            tile_kernel,
            out_shape=jax.ShapeDtypeStruct(state.shape, F32),
            grid=(blocks,),
            in_specs=[
                some,
                pl.BlockSpec((size, members), lambda n: (0, 0)),
                pl.BlockSpec((1, 1), lambda n: (0, 0)),
            ],
            out_specs=some,
            name="tile",
            interpret=INTERPRET,
            cost_estimate=pl.CostEstimate(
                flops=4 * tile_rows * size * members,
                bytes_accessed=2 * state.size * 4,
                transcendentals=0,
            ),
            compiler_params=pltpu.CompilerParams(vmem_limit_bytes=VMEM_LIMIT),
        )(state, transformed, factor)

    def move(parts, sources, dtype):
        rows = share
        return kernel_call(
            functools.partial(rows_kernel, len(parts)),
            jax.ShapeDtypeStruct((rows, members), dtype),
            [*parts, *[ref for pair in sources for ref in pair]],
            "rows",
            4 * rows * size * members * len(sources),
        )

    together = lax.optimization_barrier
    parts = scattered(pick((0,), BF16, anomalies))
    picked = [None, *[pick((colour,), F32, anomalies) for colour in range(1, NCOL)]]
    sides = [beside(obs_var, 1), beside(obs_var, -1)]
    parts[-1], picked[1], sides = together((parts[-1], picked[1], sides))
    total0 = added(parts)

    pairs = [((target,), source) for target in range(1, NCOL) for source in range(target)]
    prepared = kernel_call(
        functools.partial(setup_kernel, pairs, tiles, tile_rows),
        [jax.ShapeDtypeStruct((len(t) * share, 1), F32) for t, _ in pairs]
        + [jax.ShapeDtypeStruct((1, 1), F32)] * NCOL
        + [jax.ShapeDtypeStruct((1, size), F32)] * NCOL,
        [obs_rows, levels, place, obs_var, *sides],
        "setup",
        1_000_000,
        smem=(1, 2),
    )
    state = anomalies
    rows = total0
    done = []
    for colour in range(NCOL):
        ahead = prepared if colour == 0 else [state, *picked[colour + 1 : colour + 2]]
        whole, ahead = joined(rows, colour, ahead)
        if colour == 0:
            row_factor = {(t[0], source): out for (t, source), out in zip(pairs, ahead)}
            tile_factor = ahead[len(pairs) : len(pairs) + NCOL]
            variance = ahead[len(pairs) + NCOL :]
        else:
            state, picked[colour + 1 : colour + 2] = ahead[0], ahead[1:]
        pieces = spread(whole)
        if colour < NCOL - 1:
            coming, _ = together((picked[colour + 1], whole))
            parts = scattered(coming)
        done.append(transform(pieces, variance[colour]))
        if colour < NCOL - 1:
            sources = [(done[n], row_factor[colour + 1, n]) for n in range(colour + 1)]
            rows = move(parts, sources, BF16)
        state = move_tile(state, done[colour], tile_factor[colour], 4)
    return state


def solution(mesh):
    in_specs = (P(AXES, None), P(), P("gx", None), P())
    return jax.shard_map(
        on_device,
        mesh=mesh,
        in_specs=in_specs,
        out_specs=P(AXES, None),
        check_vma=False,
    )
```

```python
import functools

import jax
import jax.numpy as jnp
from jax import lax
from jax.experimental import pallas as pl
from jax.experimental.pallas import tpu as pltpu
from jax.sharding import PartitionSpec as P

NCOL = 4
NS_STEPS = 12
AXES = ("gx", "gy")
VMEM_LIMIT = 20 << 20
LAST_BLOCKS = 1
EXTRA = 16
INTERPRET = False
F32 = jnp.float32
BF16 = jnp.bfloat16


def kernel_call(body, out, args, name, flops, smem=(), scratch=()):
    whole = pl.BlockSpec(memory_space=pltpu.VMEM)
    scalar = pl.BlockSpec(memory_space=pltpu.SMEM)
    leaves = [*args, *jax.tree.leaves(out)]
    return pl.pallas_call(
        body,
        out_shape=out,
        in_specs=[scalar if n in smem else whole for n in range(len(args))],
        out_specs=jax.tree.map(lambda _: whole, out),
        scratch_shapes=scratch,
        name=name,
        interpret=INTERPRET,
        cost_estimate=pl.CostEstimate(
            flops=flops,
            bytes_accessed=sum(leaf.size * leaf.dtype.itemsize for leaf in leaves),
            transcendentals=0,
        ),
        compiler_params=pltpu.CompilerParams(vmem_limit_bytes=VMEM_LIMIT),
    )(*args)


def dot(left, right):
    return jnp.dot(left, right, preferred_element_type=F32)


def dot_nt(left, right):
    return lax.dot_general(
        left, right, (((1,), (1,)), ((), ())), preferred_element_type=F32
    )


def halves(value):
    high = value.astype(BF16)
    return high, (value - high.astype(F32)).astype(BF16)


def mat_prod(left, right):
    return dot(left[0], right[0]) + (dot(left[0], right[1]) + dot(left[1], right[0]))


def standing(col, colour, columns):
    offset = lax.rem(col + (NCOL - colour), NCOL)
    slot = jnp.where(offset == 1, 2, jnp.where(offset == 3, 0, 1))
    return slot, offset != 2, lax.rem(col - slot + 1 + columns, columns)


def pick_kernel(colours, state, obs, place, *refs):
    outs, scratch = refs[:-1], refs[-1]
    tiles = len(outs)
    tile_rows = state.shape[0]
    columns, size = obs.shape
    share = size // tiles
    col, tile = place[0, 0], place[0, 1]
    band = state.shape[1] // tiles
    for n, colour in enumerate(colours):
        slot, active, batch = standing(col, colour, columns)
        first = jnp.where(active, (slot * tiles + tile) * tile_rows, -(1 << 20))
        local = obs[pl.ds(batch, 1), :] - first
        row = lax.broadcasted_iota(jnp.int32, (size, size), 0)
        same = row == lax.broadcasted_iota(jnp.int32, (size, size), 1)
        wanted = jnp.sum(jnp.where(same, local.astype(F32), 0.0), axis=1, keepdims=True)
        spots = lax.broadcasted_iota(jnp.int32, (size, tile_rows), 1)
        chosen = jnp.where(spots == wanted.astype(jnp.int32), 1.0, 0.0).astype(BF16)

        def pick_band(m, _):
            lanes = pl.ds(pl.multiple_of(m * band, band), band)
            rest = state[:, lanes]
            high = rest.astype(BF16)
            picked = dot(chosen, high)
            if scratch.dtype == F32:
                rest = rest - high.astype(F32)
                middle = rest.astype(BF16)
                picked = picked + dot(chosen, middle)
                picked = picked + dot(chosen, (rest - middle.astype(F32)).astype(BF16))
            scratch[:, lanes] = picked.astype(scratch.dtype)
            return 0

        lax.fori_loop(0, tiles, pick_band, 0)
        for step, out in enumerate(outs):
            start = pl.multiple_of(lax.rem(tile + step, tiles) * share, share)
            out[n * share : (n + 1) * share, :] = scratch[pl.ds(start, share), :]


def setup_kernel(pairs, tiles, tile_rows, obs, levels, place, own, *outs):
    columns, size = obs.shape
    share = size // tiles
    col, tile = place[0, 0], place[0, 1]
    members = place[0, 2].astype(F32)
    lane = lax.broadcasted_iota(jnp.int32, (share, size), 1)
    mine = lane == lax.broadcasted_iota(jnp.int32, (share, size), 0) + tile * share

    def factor(source, which):
        slot, active, batch = standing(col, source, columns)
        level = levels[batch, slot * tiles + which].astype(F32) / 3.0
        return jnp.where(active, level, 0.0)

    for (targets, source), out in zip(pairs, outs):
        for n, target in enumerate(targets):
            slot, _, batch = standing(col, target, columns)
            inside = obs[pl.ds(batch, 1), :] - slot * (tiles * tile_rows)
            row = jnp.zeros((1, size), F32)
            for which in range(tiles):
                hit = (inside >= which * tile_rows) & (inside < (which + 1) * tile_rows)
                row = jnp.where(hit, factor(source, which), row)
            column = jnp.sum(jnp.where(mine, row, 0.0), axis=1, keepdims=True)
            out[n * share : (n + 1) * share, :] = column / members
    for colour in range(NCOL):
        outs[len(pairs) + colour][...] = jnp.full((1, 1), factor(colour, tile)) / members
    pieces = [own[:, n * share : (n + 1) * share] for n in range(tiles)]
    ordered = []
    for step in range(tiles):
        source = lax.rem(tile + tiles - step, tiles)
        piece = pieces[0]
        for n in range(1, tiles):
            piece = jnp.where(source == n, pieces[n], piece)
        ordered.append(piece)
    rest = jnp.concatenate(ordered, axis=1)
    row = lax.broadcasted_iota(jnp.int32, (EXTRA, size), 0)
    block = jnp.zeros((EXTRA, size), F32)
    for n in range(3):
        part = rest.astype(BF16).astype(F32)
        rest = rest - part
        block = jnp.where(row == n, part, block)
    for colour in range(NCOL):
        offset = lax.rem(col + (NCOL - colour), NCOL)
        sent = (offset == 0) | (offset == 2)
        out = outs[len(pairs) + NCOL + colour]
        out[...] = jnp.zeros(out.shape, BF16)
        out[:, :size] = jnp.where(sent, block, 0.0).astype(BF16)


def root_kernel(*refs):
    *pieces, variance, out = refs
    observed = jnp.concatenate([piece[...] for piece in pieces], axis=0)
    size, members = observed.shape
    row = lax.broadcasted_iota(jnp.int32, (size, size), 0)
    column = lax.broadcasted_iota(jnp.int32, (size, size), 1)
    eye = jnp.where(row == column, 1.0, 0.0).astype(F32)
    gram = dot_nt(observed, observed) / (members - 1) + eye * variance[...]
    trace = jnp.sum(jnp.sum(gram * eye, axis=1, keepdims=True), axis=0, keepdims=True)
    left = gram / trace
    right_h = halves(1.5 * eye - 0.5 * left)
    left_h = halves(mat_prod(halves(left), right_h))

    def next_term(left_h, right_h):
        return halves(1.5 * eye - 0.5 * mat_prod(right_h, left_h))

    def step(_, pair):
        left_h, right_h = pair
        term_h = next_term(left_h, right_h)
        return halves(mat_prod(left_h, term_h)), halves(mat_prod(term_h, right_h))

    left_h, right_h = lax.fori_loop(1, NS_STEPS - 1, step, (left_h, right_h))
    right = mat_prod(next_term(left_h, right_h), right_h)
    inverse_half = (right / jnp.sqrt(trace)).astype(BF16)
    out[...] = dot(inverse_half, observed).astype(BF16)


def summed(parts):
    total = parts[0][...]
    for part in parts[1:]:
        total = total + part[...]
    return total


def rows_kernel(count, *refs):
    *pairs, extra, out = refs[count:]
    rows = summed(refs[:count])
    for transformed, factor in zip(pairs[::2], pairs[1::2]):
        source = transformed[...]
        projected = dot_nt(rows.astype(BF16), source).astype(BF16)
        rows = rows - factor[...] * dot(projected, source)
    out[: rows.shape[0], :] = rows.astype(out.dtype)
    out[rows.shape[0] :, :] = extra[...]


def tile_kernel(state, transformed, factor, out):
    value = state[...]
    source = transformed[...]
    projected = dot_nt(value.astype(BF16), source).astype(BF16)
    out[...] = value - factor[...] * dot(projected, source)


def start_kernel(*refs):
    *parts, extra, out = refs
    rows = parts[0].shape[0]
    out[:rows, :] = summed(parts)
    out[rows:, :] = extra[...]


def join_kernel(*refs):
    *parts, whole, variance = refs
    total = summed(parts)
    rows, size = whole.shape[0], variance.shape[1]
    whole[...] = total[:rows]
    carried = total[rows:, :size].astype(F32)
    row = lax.broadcasted_iota(jnp.int32, carried.shape, 0)
    high, middle, low = (
        jnp.sum(jnp.where(row == n, carried, 0.0), axis=0, keepdims=True) for n in range(3)
    )
    variance[...] = (high + middle) + low


def on_device(anomalies, obs_rows, obs_var, taper_level):
    tile_rows, members = anomalies.shape
    batches, size = obs_rows.shape
    columns = lax.axis_size("gx")
    tiles = lax.axis_size("gy")
    share = size // tiles
    col = lax.axis_index("gx")
    tile = lax.axis_index("gy")
    place = jnp.stack([col, tile, jnp.int32(members - 1)]).astype(jnp.int32).reshape(1, 3)
    levels = taper_level.reshape(batches, 3 * tiles)
    everywhere = list(range(columns))

    def hop(value, pairs):
        flat = [
            ((a % columns) * tiles + b % tiles, (c % columns) * tiles + d % tiles)
            for (a, b), (c, d) in pairs
        ]
        return lax.ppermute(value, AXES, flat)

    def along_gy(value, step):
        return hop(value, [((c, n), (c, n + step)) for c in everywhere for n in range(tiles)])

    def along_gx(value, colour, step):
        trio = (-1, 0, 1)
        pairs = [
            ((b + trio[m], n), (b + trio[(m + step) % 3], n))
            for b in range(colour, columns, NCOL)
            for m in range(3)
            for n in range(tiles)
        ]
        pairs += [
            ((b + 2, n), (b + 2, n + 1 - 2 * (n % 2)))
            for b in range(colour, columns, NCOL)
            for n in range(tiles)
        ]
        return hop(value, pairs)

    def pick(colours, dtype, state):
        shape = jax.ShapeDtypeStruct((len(colours) * share, members), dtype)
        return kernel_call(
            functools.partial(pick_kernel, colours),
            [shape] * tiles,
            [state, obs_rows, place],
            "pick",
            2 * size * tile_rows * members * len(colours) * (1 if dtype == BF16 else 3),
            smem=(2,),
            scratch=[pltpu.VMEM((size, members), dtype)],
        )

    def scattered(parts):
        return [parts[0], *[along_gy(parts[n], n) for n in range(1, tiles)]]

    def joined(rows, colour, beside_it):
        first, second = (along_gx(rows, colour, step) for step in (1, 2))
        second, beside_it = lax.optimization_barrier((second, beside_it))
        shapes = [
            jax.ShapeDtypeStruct((share, members), BF16),
            jax.ShapeDtypeStruct((1, size), F32),
        ]
        args = [rows, first, second]
        return *kernel_call(join_kernel, shapes, args, "join", 1_000_000), beside_it

    def spread(whole):
        return [whole, *[along_gy(whole, step) for step in range(1, tiles)]]

    def transform(pieces, variance):
        return kernel_call(
            root_kernel,
            jax.ShapeDtypeStruct((size, members), BF16),
            [*pieces, variance],
            "root",
            8_000_000_000,
        )

    def move_tile(state, transformed, factor, blocks):
        some = pl.BlockSpec((tile_rows // blocks, members), lambda n: (n, 0))
        return pl.pallas_call(
            tile_kernel,
            out_shape=jax.ShapeDtypeStruct(state.shape, F32),
            grid=(blocks,),
            in_specs=[
                some,
                pl.BlockSpec((size, members), lambda n: (0, 0)),
                pl.BlockSpec((1, 1), lambda n: (0, 0)),
            ],
            out_specs=some,
            name="tile",
            interpret=INTERPRET,
            cost_estimate=pl.CostEstimate(
                flops=4 * tile_rows * size * members,
                bytes_accessed=2 * state.size * 4,
                transcendentals=0,
            ),
            compiler_params=pltpu.CompilerParams(vmem_limit_bytes=VMEM_LIMIT),
        )(state, transformed, factor)

    def move(parts, sources, extra):
        rows = share
        return kernel_call(
            functools.partial(rows_kernel, len(parts)),
            jax.ShapeDtypeStruct((rows + EXTRA, members), BF16),
            [*parts, *[ref for pair in sources for ref in pair], extra],
            "rows",
            4 * rows * size * members * len(sources),
        )

    parts = scattered(pick((0,), BF16, anomalies))
    picked = [None, *[pick((colour,), F32, anomalies) for colour in range(1, NCOL)]]
    pairs = [((target,), source) for target in range(1, NCOL) for source in range(target)]
    prepared = kernel_call(
        functools.partial(setup_kernel, pairs, tiles, tile_rows),
        [jax.ShapeDtypeStruct((len(t) * share, 1), F32) for t, _ in pairs]
        + [jax.ShapeDtypeStruct((1, 1), F32)] * NCOL
        + [jax.ShapeDtypeStruct((EXTRA, members), BF16)] * NCOL,
        [obs_rows, levels, place, obs_var],
        "setup",
        1_000_000,
        smem=(1, 2),
    )
    row_factor = {(t[0], source): out for (t, source), out in zip(pairs, prepared)}
    tile_factor = prepared[len(pairs) : len(pairs) + NCOL]
    extra = prepared[len(pairs) + NCOL :]
    parts[-1], picked[1] = lax.optimization_barrier((parts[-1], picked[1]))
    rows = kernel_call(
        start_kernel,
        jax.ShapeDtypeStruct((share + EXTRA, members), BF16),
        [*parts, extra[0]],
        "start",
        1_000_000,
    )

    state = anomalies
    done = []
    for colour in range(NCOL):
        if colour == 0:
            whole, variance, picked[2:] = joined(rows, colour, picked[2:])
        else:
            whole, variance, state = joined(rows, colour, state)
        pieces = spread(whole)
        if colour < NCOL - 1:
            coming, _ = lax.optimization_barrier((picked[colour + 1], whole))
            parts = scattered(coming)
        done.append(transform(pieces, variance))
        if colour < NCOL - 1:
            sources = [(done[n], row_factor[colour + 1, n]) for n in range(colour + 1)]
            rows = move(parts, sources, extra[colour + 1])
        blocks = 4 if colour < NCOL - 1 else LAST_BLOCKS
        state = move_tile(state, done[colour], tile_factor[colour], blocks)
    return state


def solution(mesh):
    in_specs = (P(AXES, None), P(), P("gx", None), P())
    return jax.shard_map(
        on_device,
        mesh=mesh,
        in_specs=in_specs,
        out_specs=P(AXES, None),
        check_vma=False,
    )
```

```python
import functools

import jax
import jax.numpy as jnp
from jax import lax
from jax.experimental import pallas as pl
from jax.experimental.pallas import tpu as pltpu
from jax.sharding import PartitionSpec as P

NCOL = 4
NS_STEPS = 12
AXES = ("gx", "gy")
VMEM_LIMIT = 20 << 20
LAST_BLOCKS = 1
EXTRA = 16
INTERPRET = False
F32 = jnp.float32
BF16 = jnp.bfloat16


def kernel_call(body, out, args, name, flops, smem=(), scratch=()):
    whole = pl.BlockSpec(memory_space=pltpu.VMEM)
    scalar = pl.BlockSpec(memory_space=pltpu.SMEM)
    leaves = [*args, *jax.tree.leaves(out)]
    return pl.pallas_call(
        body,
        out_shape=out,
        in_specs=[scalar if n in smem else whole for n in range(len(args))],
        out_specs=jax.tree.map(lambda _: whole, out),
        scratch_shapes=scratch,
        name=name,
        interpret=INTERPRET,
        cost_estimate=pl.CostEstimate(
            flops=flops,
            bytes_accessed=sum(leaf.size * leaf.dtype.itemsize for leaf in leaves),
            transcendentals=0,
        ),
        compiler_params=pltpu.CompilerParams(vmem_limit_bytes=VMEM_LIMIT),
    )(*args)


def dot(left, right):
    return jnp.dot(left, right, preferred_element_type=F32)


def dot_nt(left, right):
    return lax.dot_general(
        left, right, (((1,), (1,)), ((), ())), preferred_element_type=F32
    )


def halves(value):
    high = value.astype(BF16)
    return high, (value - high.astype(F32)).astype(BF16)


def mat_prod(left, right):
    return dot(left[0], right[0]) + (dot(left[0], right[1]) + dot(left[1], right[0]))


def standing(col, colour, columns):
    offset = lax.rem(col + (NCOL - colour), NCOL)
    slot = jnp.where(offset == 1, 2, jnp.where(offset == 3, 0, 1))
    return slot, offset != 2, lax.rem(col - slot + 1 + columns, columns)


def pick_kernel(colours, state, obs, place, *refs):
    outs, scratch = refs[:-1], refs[-1]
    tiles = len(outs)
    tile_rows = state.shape[0]
    columns, size = obs.shape
    share = size // tiles
    col, tile = place[0, 0], place[0, 1]
    band = state.shape[1] // tiles
    for n, colour in enumerate(colours):
        slot, active, batch = standing(col, colour, columns)
        first = jnp.where(active, (slot * tiles + tile) * tile_rows, -(1 << 20))
        local = obs[pl.ds(batch, 1), :] - first
        row = lax.broadcasted_iota(jnp.int32, (size, size), 0)
        same = row == lax.broadcasted_iota(jnp.int32, (size, size), 1)
        wanted = jnp.sum(jnp.where(same, local.astype(F32), 0.0), axis=1, keepdims=True)
        spots = lax.broadcasted_iota(jnp.int32, (size, tile_rows), 1)
        chosen = jnp.where(spots == wanted.astype(jnp.int32), 1.0, 0.0).astype(BF16)

        def pick_band(m, _):
            lanes = pl.ds(pl.multiple_of(m * band, band), band)
            rest = state[:, lanes]
            high = rest.astype(BF16)
            picked = dot(chosen, high)
            if scratch.dtype == F32:
                rest = rest - high.astype(F32)
                middle = rest.astype(BF16)
                picked = picked + dot(chosen, middle)
                picked = picked + dot(chosen, (rest - middle.astype(F32)).astype(BF16))
            scratch[:, lanes] = picked.astype(scratch.dtype)
            return 0

        lax.fori_loop(0, tiles, pick_band, 0)
        for step, out in enumerate(outs):
            start = pl.multiple_of(lax.rem(tile + step, tiles) * share, share)
            out[n * share : (n + 1) * share, :] = scratch[pl.ds(start, share), :]


def setup_kernel(pairs, tiles, tile_rows, obs, levels, place, own, *outs):
    columns, size = obs.shape
    share = size // tiles
    col, tile = place[0, 0], place[0, 1]
    members = place[0, 2].astype(F32)
    lane = lax.broadcasted_iota(jnp.int32, (share, size), 1)
    mine = lane == lax.broadcasted_iota(jnp.int32, (share, size), 0) + tile * share

    def factor(source, which):
        slot, active, batch = standing(col, source, columns)
        level = levels[batch, slot * tiles + which].astype(F32) / 3.0
        return jnp.where(active, level, 0.0)

    for (targets, source), out in zip(pairs, outs):
        for n, target in enumerate(targets):
            slot, _, batch = standing(col, target, columns)
            inside = obs[pl.ds(batch, 1), :] - slot * (tiles * tile_rows)
            row = jnp.zeros((1, size), F32)
            for which in range(tiles):
                hit = (inside >= which * tile_rows) & (inside < (which + 1) * tile_rows)
                row = jnp.where(hit, factor(source, which), row)
            column = jnp.sum(jnp.where(mine, row, 0.0), axis=1, keepdims=True)
            out[n * share : (n + 1) * share, :] = column / members
    for colour in range(NCOL):
        outs[len(pairs) + colour][...] = jnp.full((1, 1), factor(colour, tile)) / members
    pieces = [own[:, n * share : (n + 1) * share] for n in range(tiles)]
    ordered = []
    for step in range(tiles):
        source = lax.rem(tile + tiles - step, tiles)
        piece = pieces[0]
        for n in range(1, tiles):
            piece = jnp.where(source == n, pieces[n], piece)
        ordered.append(piece)
    rest = jnp.concatenate(ordered, axis=1)
    row = lax.broadcasted_iota(jnp.int32, (EXTRA, size), 0)
    block = jnp.zeros((EXTRA, size), F32)
    for n in range(3):
        part = rest.astype(BF16).astype(F32)
        rest = rest - part
        block = jnp.where(row == n, part, block)
    for colour in range(NCOL):
        offset = lax.rem(col + (NCOL - colour), NCOL)
        sent = (offset == 0) | (offset == 2)
        out = outs[len(pairs) + NCOL + colour]
        out[...] = jnp.zeros(out.shape, BF16)
        out[:, :size] = jnp.where(sent, block, 0.0).astype(BF16)


def root_kernel(*refs):
    *pieces, variance, out = refs
    observed = jnp.concatenate([piece[...] for piece in pieces], axis=0)
    size, members = observed.shape
    row = lax.broadcasted_iota(jnp.int32, (size, size), 0)
    column = lax.broadcasted_iota(jnp.int32, (size, size), 1)
    eye = jnp.where(row == column, 1.0, 0.0).astype(F32)
    gram = dot_nt(observed, observed) / (members - 1) + eye * variance[...]
    trace = jnp.sum(jnp.sum(gram * eye, axis=1, keepdims=True), axis=0, keepdims=True)
    left = gram / trace
    right_h = halves(1.5 * eye - 0.5 * left)
    left_h = halves(mat_prod(halves(left), right_h))

    def next_term(left_h, right_h):
        return halves(1.5 * eye - 0.5 * mat_prod(right_h, left_h))

    def step(_, pair):
        left_h, right_h = pair
        term_h = next_term(left_h, right_h)
        return halves(mat_prod(left_h, term_h)), halves(mat_prod(term_h, right_h))

    left_h, right_h = lax.fori_loop(1, NS_STEPS - 1, step, (left_h, right_h))
    right = mat_prod(next_term(left_h, right_h), right_h)
    inverse_half = (right / jnp.sqrt(trace)).astype(BF16)
    out[...] = dot(inverse_half, observed).astype(BF16)


def summed(parts):
    total = parts[0][...]
    for part in parts[1:]:
        total = total + part[...]
    return total


def rows_kernel(count, *refs):
    *pairs, extra, out = refs[count:]
    rows = summed(refs[:count])
    for transformed, factor in zip(pairs[::2], pairs[1::2]):
        source = transformed[...]
        projected = dot_nt(rows.astype(BF16), source).astype(BF16)
        rows = rows - factor[...] * dot(projected, source)
    out[: rows.shape[0], :] = rows.astype(out.dtype)
    out[rows.shape[0] :, :] = extra[...]


def tile_kernel(state, transformed, factor, out):
    value = state[...]
    source = transformed[...]
    projected = dot_nt(value.astype(BF16), source).astype(BF16)
    out[...] = value - factor[...] * dot(projected, source)


def start_kernel(*refs):
    *parts, extra, out = refs
    rows = parts[0].shape[0]
    out[:rows, :] = summed(parts)
    out[rows:, :] = extra[...]


def join_kernel(*refs):
    *parts, whole, variance = refs
    total = summed(parts)
    rows, size = whole.shape[0], variance.shape[1]
    whole[...] = total[:rows]
    carried = total[rows:, :size].astype(F32)
    row = lax.broadcasted_iota(jnp.int32, carried.shape, 0)
    high, middle, low = (
        jnp.sum(jnp.where(row == n, carried, 0.0), axis=0, keepdims=True) for n in range(3)
    )
    variance[...] = (high + middle) + low


def on_device(anomalies, obs_rows, obs_var, taper_level):
    tile_rows, members = anomalies.shape
    batches, size = obs_rows.shape
    columns = lax.axis_size("gx")
    tiles = lax.axis_size("gy")
    share = size // tiles
    col = lax.axis_index("gx")
    tile = lax.axis_index("gy")
    place = jnp.stack([col, tile, jnp.int32(members - 1)]).astype(jnp.int32).reshape(1, 3)
    levels = taper_level.reshape(batches, 3 * tiles)
    everywhere = list(range(columns))

    def hop(value, pairs):
        flat = [
            ((a % columns) * tiles + b % tiles, (c % columns) * tiles + d % tiles)
            for (a, b), (c, d) in pairs
        ]
        return lax.ppermute(value, AXES, flat)

    def along_gy(value, step):
        return hop(value, [((c, n), (c, n + step)) for c in everywhere for n in range(tiles)])

    def along_gx(value, colour, step):
        trio = (-1, 0, 1)
        pairs = [
            ((b + trio[m], n), (b + trio[(m + step) % 3], n))
            for b in range(colour, columns, NCOL)
            for m in range(3)
            for n in range(tiles)
        ]
        pairs += [
            ((b + 2, n), (b + 2, n + 1 - 2 * (n % 2)))
            for b in range(colour, columns, NCOL)
            for n in range(tiles)
        ]
        return hop(value, pairs)

    def pick(colours, dtype, state):
        shape = jax.ShapeDtypeStruct((len(colours) * share, members), dtype)
        return kernel_call(
            functools.partial(pick_kernel, colours),
            [shape] * tiles,
            [state, obs_rows, place],
            "pick",
            2 * size * tile_rows * members * len(colours) * (1 if dtype == BF16 else 3),
            smem=(2,),
            scratch=[pltpu.VMEM((size, members), dtype)],
        )

    def scattered(parts):
        return [parts[0], *[along_gy(parts[n], n) for n in range(1, tiles)]]

    def joined(rows, colour, beside_it):
        first, second = (along_gx(rows, colour, step) for step in (1, 2))
        second, beside_it = lax.optimization_barrier((second, beside_it))
        shapes = [
            jax.ShapeDtypeStruct((share, members), BF16),
            jax.ShapeDtypeStruct((1, size), F32),
        ]
        args = [rows, first, second]
        return *kernel_call(join_kernel, shapes, args, "join", 1_000_000), beside_it

    def spread(whole):
        return [whole, *[along_gy(whole, step) for step in range(1, tiles)]]

    def transform(pieces, variance):
        return kernel_call(
            root_kernel,
            jax.ShapeDtypeStruct((size, members), BF16),
            [*pieces, variance],
            "root",
            8_000_000_000,
        )

    def move_tile(state, transformed, factor, blocks):
        some = pl.BlockSpec((tile_rows // blocks, members), lambda n: (n, 0))
        return pl.pallas_call(
            tile_kernel,
            out_shape=jax.ShapeDtypeStruct(state.shape, F32),
            grid=(blocks,),
            in_specs=[
                some,
                pl.BlockSpec((size, members), lambda n: (0, 0)),
                pl.BlockSpec((1, 1), lambda n: (0, 0)),
            ],
            out_specs=some,
            name="tile",
            interpret=INTERPRET,
            cost_estimate=pl.CostEstimate(
                flops=4 * tile_rows * size * members,
                bytes_accessed=2 * state.size * 4,
                transcendentals=0,
            ),
            compiler_params=pltpu.CompilerParams(vmem_limit_bytes=VMEM_LIMIT),
        )(state, transformed, factor)

    def move(parts, sources, extra):
        rows = share
        return kernel_call(
            functools.partial(rows_kernel, len(parts)),
            jax.ShapeDtypeStruct((rows + EXTRA, members), BF16),
            [*parts, *[ref for pair in sources for ref in pair], extra],
            "rows",
            4 * rows * size * members * len(sources),
        )

    parts = scattered(pick((0,), BF16, anomalies))
    picked = [None, *[pick((colour,), F32, anomalies) for colour in range(1, NCOL)]]
    pairs = [((target,), source) for target in range(1, NCOL) for source in range(target)]
    prepared = kernel_call(
        functools.partial(setup_kernel, pairs, tiles, tile_rows),
        [jax.ShapeDtypeStruct((len(t) * share, 1), F32) for t, _ in pairs]
        + [jax.ShapeDtypeStruct((1, 1), F32)] * NCOL
        + [jax.ShapeDtypeStruct((EXTRA, members), BF16)] * NCOL,
        [obs_rows, levels, place, obs_var],
        "setup",
        1_000_000,
        smem=(1, 2),
    )
    row_factor = {(t[0], source): out for (t, source), out in zip(pairs, prepared)}
    tile_factor = prepared[len(pairs) : len(pairs) + NCOL]
    extra = prepared[len(pairs) + NCOL :]
    parts[-1], picked[1] = lax.optimization_barrier((parts[-1], picked[1]))
    rows = kernel_call(
        start_kernel,
        jax.ShapeDtypeStruct((share + EXTRA, members), BF16),
        [*parts, extra[0]],
        "start",
        1_000_000,
    )

    state = anomalies
    done = []
    for colour in range(NCOL):
        if colour < NCOL - 1:
            coming, rows = lax.optimization_barrier((picked[colour + 1], rows))
            parts = scattered(coming)
        whole, variance, picked[colour + 2 :] = joined(rows, colour, picked[colour + 2 :])
        pieces = spread(whole)
        if colour > 0:
            pieces[-1], state = lax.optimization_barrier((pieces[-1], state))
        if colour < NCOL - 1:
            pieces[-1], parts = lax.optimization_barrier((pieces[-1], parts))
        done.append(transform(pieces, variance))
        if colour < NCOL - 1:
            sources = [(done[n], row_factor[colour + 1, n]) for n in range(colour + 1)]
            rows = move(parts, sources, extra[colour + 1])
        blocks = 4 if colour < NCOL - 1 else LAST_BLOCKS
        state = move_tile(state, done[colour], tile_factor[colour], blocks)
    return state


def solution(mesh):
    in_specs = (P(AXES, None), P(), P("gx", None), P())
    return jax.shard_map(
        on_device,
        mesh=mesh,
        in_specs=in_specs,
        out_specs=P(AXES, None),
        check_vma=False,
    )
```

```python
import functools

import jax
import jax.numpy as jnp
from jax import lax
from jax.experimental import pallas as pl
from jax.experimental.pallas import tpu as pltpu
from jax.sharding import PartitionSpec as P

NCOL = 4
NS_STEPS = 12
AXES = ("gx", "gy")
VMEM_LIMIT = 20 << 20
LAST_BLOCKS = 1
EXTRA = 16
INTERPRET = False
F32 = jnp.float32
BF16 = jnp.bfloat16


def kernel_call(body, out, args, name, flops, smem=(), scratch=()):
    whole = pl.BlockSpec(memory_space=pltpu.VMEM)
    scalar = pl.BlockSpec(memory_space=pltpu.SMEM)
    leaves = [*args, *jax.tree.leaves(out)]
    return pl.pallas_call(
        body,
        out_shape=out,
        in_specs=[scalar if n in smem else whole for n in range(len(args))],
        out_specs=jax.tree.map(lambda _: whole, out),
        scratch_shapes=scratch,
        name=name,
        interpret=INTERPRET,
        cost_estimate=pl.CostEstimate(
            flops=flops,
            bytes_accessed=sum(leaf.size * leaf.dtype.itemsize for leaf in leaves),
            transcendentals=0,
        ),
        compiler_params=pltpu.CompilerParams(vmem_limit_bytes=VMEM_LIMIT),
    )(*args)


def dot(left, right):
    return jnp.dot(left, right, preferred_element_type=F32)


def dot_nt(left, right):
    return lax.dot_general(
        left, right, (((1,), (1,)), ((), ())), preferred_element_type=F32
    )


def halves(value):
    high = value.astype(BF16)
    return high, (value - high.astype(F32)).astype(BF16)


def mat_prod(left, right):
    return dot(left[0], right[0]) + (dot(left[0], right[1]) + dot(left[1], right[0]))


def standing(col, colour, columns):
    offset = lax.rem(col + (NCOL - colour), NCOL)
    slot = jnp.where(offset == 1, 2, jnp.where(offset == 3, 0, 1))
    return slot, offset != 2, lax.rem(col - slot + 1 + columns, columns)


def pick_kernel(colours, state, obs, place, *refs):
    outs, scratch = refs[:-1], refs[-1]
    tiles = len(outs)
    tile_rows = state.shape[0]
    columns, size = obs.shape
    share = size // tiles
    col, tile = place[0, 0], place[0, 1]
    bands = tiles if scratch.dtype == F32 else 1
    band = state.shape[1] // bands
    for n, colour in enumerate(colours):
        slot, active, batch = standing(col, colour, columns)
        first = jnp.where(active, (slot * tiles + tile) * tile_rows, -(1 << 20))
        local = obs[pl.ds(batch, 1), :] - first
        row = lax.broadcasted_iota(jnp.int32, (size, size), 0)
        same = row == lax.broadcasted_iota(jnp.int32, (size, size), 1)
        wanted = jnp.sum(jnp.where(same, local.astype(F32), 0.0), axis=1, keepdims=True)
        spots = lax.broadcasted_iota(jnp.int32, (size, tile_rows), 1)
        chosen = jnp.where(spots == wanted.astype(jnp.int32), 1.0, 0.0).astype(BF16)

        def pick_band(m, _):
            lanes = pl.ds(pl.multiple_of(m * band, band), band)
            rest = state[:, lanes]
            high = rest.astype(BF16)
            picked = dot(chosen, high)
            if scratch.dtype == F32:
                rest = rest - high.astype(F32)
                middle = rest.astype(BF16)
                picked = picked + dot(chosen, middle)
                picked = picked + dot(chosen, (rest - middle.astype(F32)).astype(BF16))
            scratch[:, lanes] = picked.astype(scratch.dtype)
            return 0

        lax.fori_loop(0, bands, pick_band, 0)
        for step, out in enumerate(outs):
            start = pl.multiple_of(lax.rem(tile + step, tiles) * share, share)
            out[n * share : (n + 1) * share, :] = scratch[pl.ds(start, share), :]


def setup_kernel(pairs, tiles, tile_rows, obs, levels, place, own, *outs):
    columns, size = obs.shape
    share = size // tiles
    col, tile = place[0, 0], place[0, 1]
    members = place[0, 2].astype(F32)
    lane = lax.broadcasted_iota(jnp.int32, (share, size), 1)
    mine = lane == lax.broadcasted_iota(jnp.int32, (share, size), 0) + tile * share

    def factor(source, which):
        slot, active, batch = standing(col, source, columns)
        level = levels[batch, slot * tiles + which].astype(F32) / 3.0
        return jnp.where(active, level, 0.0)

    for (targets, source), out in zip(pairs, outs):
        for n, target in enumerate(targets):
            slot, _, batch = standing(col, target, columns)
            inside = obs[pl.ds(batch, 1), :] - slot * (tiles * tile_rows)
            row = jnp.zeros((1, size), F32)
            for which in range(tiles):
                hit = (inside >= which * tile_rows) & (inside < (which + 1) * tile_rows)
                row = jnp.where(hit, factor(source, which), row)
            column = jnp.sum(jnp.where(mine, row, 0.0), axis=1, keepdims=True)
            out[n * share : (n + 1) * share, :] = column / members
    for colour in range(NCOL):
        outs[len(pairs) + colour][...] = jnp.full((1, 1), factor(colour, tile)) / members
    pieces = [own[:, n * share : (n + 1) * share] for n in range(tiles)]
    ordered = []
    for step in range(tiles):
        source = lax.rem(tile + tiles - step, tiles)
        piece = pieces[0]
        for n in range(1, tiles):
            piece = jnp.where(source == n, pieces[n], piece)
        ordered.append(piece)
    rest = jnp.concatenate(ordered, axis=1)
    row = lax.broadcasted_iota(jnp.int32, (EXTRA, size), 0)
    block = jnp.zeros((EXTRA, size), F32)
    for n in range(3):
        part = rest.astype(BF16).astype(F32)
        rest = rest - part
        block = jnp.where(row == n, part, block)
    for colour in range(NCOL):
        offset = lax.rem(col + (NCOL - colour), NCOL)
        sent = (offset == 0) | (offset == 2)
        out = outs[len(pairs) + NCOL + colour]
        out[...] = jnp.zeros(out.shape, BF16)
        out[:, :size] = jnp.where(sent, block, 0.0).astype(BF16)


def root_kernel(*refs):
    *pieces, variance, out = refs
    observed = jnp.concatenate([piece[...] for piece in pieces], axis=0)
    size, members = observed.shape
    row = lax.broadcasted_iota(jnp.int32, (size, size), 0)
    column = lax.broadcasted_iota(jnp.int32, (size, size), 1)
    eye = jnp.where(row == column, 1.0, 0.0).astype(F32)
    gram = dot_nt(observed, observed) / (members - 1) + eye * variance[...]
    trace = jnp.sum(jnp.sum(gram * eye, axis=1, keepdims=True), axis=0, keepdims=True)
    left = gram / trace
    right_h = halves(1.5 * eye - 0.5 * left)
    left_h = halves(mat_prod(halves(left), right_h))

    def next_term(left_h, right_h):
        return halves(1.5 * eye - 0.5 * mat_prod(right_h, left_h))

    def step(_, pair):
        left_h, right_h = pair
        term_h = next_term(left_h, right_h)
        return halves(mat_prod(left_h, term_h)), halves(mat_prod(term_h, right_h))

    left_h, right_h = lax.fori_loop(1, NS_STEPS - 1, step, (left_h, right_h))
    right = mat_prod(next_term(left_h, right_h), right_h)
    inverse_half = (right / jnp.sqrt(trace)).astype(BF16)
    out[...] = dot(inverse_half, observed).astype(BF16)


def summed(parts):
    total = parts[0][...]
    for part in parts[1:]:
        total = total + part[...]
    return total


def rows_kernel(count, *refs):
    *pairs, extra, out = refs[count:]
    rows = summed(refs[:count])
    for transformed, factor in zip(pairs[::2], pairs[1::2]):
        source = transformed[...]
        projected = dot_nt(rows.astype(BF16), source).astype(BF16)
        rows = rows - factor[...] * dot(projected, source)
    out[: rows.shape[0], :] = rows.astype(out.dtype)
    out[rows.shape[0] :, :] = extra[...]


def tile_kernel(state, transformed, factor, out):
    value = state[...]
    source = transformed[...]
    projected = dot_nt(value.astype(BF16), source).astype(BF16)
    out[...] = value - factor[...] * dot(projected, source)


def start_kernel(*refs):
    *parts, extra, out = refs
    rows = parts[0].shape[0]
    out[:rows, :] = summed(parts)
    out[rows:, :] = extra[...]


def join_kernel(*refs):
    *parts, whole, variance = refs
    total = summed(parts)
    rows, size = whole.shape[0], variance.shape[1]
    whole[...] = total[:rows]
    carried = total[rows:, :size].astype(F32)
    row = lax.broadcasted_iota(jnp.int32, carried.shape, 0)
    high, middle, low = (
        jnp.sum(jnp.where(row == n, carried, 0.0), axis=0, keepdims=True) for n in range(3)
    )
    variance[...] = (high + middle) + low


def on_device(anomalies, obs_rows, obs_var, taper_level):
    tile_rows, members = anomalies.shape
    batches, size = obs_rows.shape
    columns = lax.axis_size("gx")
    tiles = lax.axis_size("gy")
    share = size // tiles
    col = lax.axis_index("gx")
    tile = lax.axis_index("gy")
    place = jnp.stack([col, tile, jnp.int32(members - 1)]).astype(jnp.int32).reshape(1, 3)
    levels = taper_level.reshape(batches, 3 * tiles)
    everywhere = list(range(columns))

    def hop(value, pairs):
        flat = [
            ((a % columns) * tiles + b % tiles, (c % columns) * tiles + d % tiles)
            for (a, b), (c, d) in pairs
        ]
        return lax.ppermute(value, AXES, flat)

    def along_gy(value, step):
        return hop(value, [((c, n), (c, n + step)) for c in everywhere for n in range(tiles)])

    def along_gx(value, colour, step):
        trio = (-1, 0, 1)
        pairs = [
            ((b + trio[m], n), (b + trio[(m + step) % 3], n))
            for b in range(colour, columns, NCOL)
            for m in range(3)
            for n in range(tiles)
        ]
        pairs += [
            ((b + 2, n), (b + 2, n + 1 - 2 * (n % 2)))
            for b in range(colour, columns, NCOL)
            for n in range(tiles)
        ]
        return hop(value, pairs)

    def pick(colours, dtype, state):
        shape = jax.ShapeDtypeStruct((len(colours) * share, members), dtype)
        return kernel_call(
            functools.partial(pick_kernel, colours),
            [shape] * tiles,
            [state, obs_rows, place],
            "pick",
            2 * size * tile_rows * members * len(colours) * (1 if dtype == BF16 else 3),
            smem=(2,),
            scratch=[pltpu.VMEM((size, members), dtype)],
        )

    def scattered(parts):
        return [parts[0], *[along_gy(parts[n], n) for n in range(1, tiles)]]

    def joined(rows, colour, beside_it):
        first, second = (along_gx(rows, colour, step) for step in (1, 2))
        second, beside_it = lax.optimization_barrier((second, beside_it))
        shapes = [
            jax.ShapeDtypeStruct((share, members), BF16),
            jax.ShapeDtypeStruct((1, size), F32),
        ]
        args = [rows, first, second]
        return *kernel_call(join_kernel, shapes, args, "join", 1_000_000), beside_it

    def spread(whole):
        return [whole, *[along_gy(whole, step) for step in range(1, tiles)]]

    def transform(pieces, variance):
        return kernel_call(
            root_kernel,
            jax.ShapeDtypeStruct((size, members), BF16),
            [*pieces, variance],
            "root",
            8_000_000_000,
        )

    def move_tile(state, transformed, factor, blocks):
        some = pl.BlockSpec((tile_rows // blocks, members), lambda n: (n, 0))
        return pl.pallas_call(
            tile_kernel,
            out_shape=jax.ShapeDtypeStruct(state.shape, F32),
            grid=(blocks,),
            in_specs=[
                some,
                pl.BlockSpec((size, members), lambda n: (0, 0)),
                pl.BlockSpec((1, 1), lambda n: (0, 0)),
            ],
            out_specs=some,
            name="tile",
            interpret=INTERPRET,
            cost_estimate=pl.CostEstimate(
                flops=4 * tile_rows * size * members,
                bytes_accessed=2 * state.size * 4,
                transcendentals=0,
            ),
            compiler_params=pltpu.CompilerParams(vmem_limit_bytes=VMEM_LIMIT),
        )(state, transformed, factor)

    def move(parts, sources, extra):
        rows = share
        return kernel_call(
            functools.partial(rows_kernel, len(parts)),
            jax.ShapeDtypeStruct((rows + EXTRA, members), BF16),
            [*parts, *[ref for pair in sources for ref in pair], extra],
            "rows",
            4 * rows * size * members * len(sources),
        )

    parts = scattered(pick((0,), BF16, anomalies))
    picked = [None, *[pick((colour,), F32, anomalies) for colour in range(1, NCOL)]]
    pairs = [((target,), source) for target in range(1, NCOL) for source in range(target)]
    prepared = kernel_call(
        functools.partial(setup_kernel, pairs, tiles, tile_rows),
        [jax.ShapeDtypeStruct((len(t) * share, 1), F32) for t, _ in pairs]
        + [jax.ShapeDtypeStruct((1, 1), F32)] * NCOL
        + [jax.ShapeDtypeStruct((EXTRA, members), BF16)] * NCOL,
        [obs_rows, levels, place, obs_var],
        "setup",
        1_000_000,
        smem=(1, 2),
    )
    row_factor = {(t[0], source): out for (t, source), out in zip(pairs, prepared)}
    tile_factor = prepared[len(pairs) : len(pairs) + NCOL]
    extra = prepared[len(pairs) + NCOL :]
    parts[-1], picked[1] = lax.optimization_barrier((parts[-1], picked[1]))
    rows = kernel_call(
        start_kernel,
        jax.ShapeDtypeStruct((share + EXTRA, members), BF16),
        [*parts, extra[0]],
        "start",
        1_000_000,
    )

    state = anomalies
    done = []
    for colour in range(NCOL):
        ahead = picked[2:] if colour == 0 else [state]
        if colour < NCOL - 1:
            coming, rows = lax.optimization_barrier((picked[colour + 1], rows))
            ahead = [*ahead, along_gy(coming[1], 1)]
        whole, variance, ahead = joined(rows, colour, ahead)
        if colour == 0:
            picked[2:] = ahead[:2]
        else:
            state = ahead[0]
        pieces = spread(whole)
        if colour < NCOL - 1:
            late, _ = lax.optimization_barrier((coming, whole))
            parts = [coming[0], ahead[-1], *[along_gy(late[n], n) for n in (2, 3)]]
        done.append(transform(pieces, variance))
        if colour < NCOL - 1:
            sources = [(done[n], row_factor[colour + 1, n]) for n in range(colour + 1)]
            rows = move(parts, sources, extra[colour + 1])
        blocks = 4 if colour < NCOL - 1 else LAST_BLOCKS
        state = move_tile(state, done[colour], tile_factor[colour], blocks)
    return state


def solution(mesh):
    in_specs = (P(AXES, None), P(), P("gx", None), P())
    return jax.shard_map(
        on_device,
        mesh=mesh,
        in_specs=in_specs,
        out_specs=P(AXES, None),
        check_vma=False,
    )
```

```python
import functools

import jax
import jax.numpy as jnp
from jax import lax
from jax.experimental import pallas as pl
from jax.experimental.pallas import tpu as pltpu
from jax.sharding import PartitionSpec as P

NCOL = 4
NS_STEPS = 12
AXES = ("gx", "gy")
VMEM_LIMIT = 20 << 20
LAST_BLOCKS = 1
EXTRA = 16
INTERPRET = False
F32 = jnp.float32
BF16 = jnp.bfloat16


def kernel_call(body, out, args, name, flops, smem=(), scratch=()):
    whole = pl.BlockSpec(memory_space=pltpu.VMEM)
    scalar = pl.BlockSpec(memory_space=pltpu.SMEM)
    leaves = [*args, *jax.tree.leaves(out)]
    return pl.pallas_call(
        body,
        out_shape=out,
        in_specs=[scalar if n in smem else whole for n in range(len(args))],
        out_specs=jax.tree.map(lambda _: whole, out),
        scratch_shapes=scratch,
        name=name,
        interpret=INTERPRET,
        cost_estimate=pl.CostEstimate(
            flops=flops,
            bytes_accessed=sum(leaf.size * leaf.dtype.itemsize for leaf in leaves),
            transcendentals=0,
        ),
        compiler_params=pltpu.CompilerParams(vmem_limit_bytes=VMEM_LIMIT),
    )(*args)


def dot(left, right):
    return jnp.dot(left, right, preferred_element_type=F32)


def dot_nt(left, right):
    return lax.dot_general(
        left, right, (((1,), (1,)), ((), ())), preferred_element_type=F32
    )


def halves(value):
    high = value.astype(BF16)
    return high, (value - high.astype(F32)).astype(BF16)


def mat_prod(left, right):
    return dot(left[0], right[0]) + (dot(left[0], right[1]) + dot(left[1], right[0]))


def standing(col, colour, columns):
    offset = lax.rem(col + (NCOL - colour), NCOL)
    slot = jnp.where(offset == 1, 2, jnp.where(offset == 3, 0, 1))
    return slot, offset != 2, lax.rem(col - slot + 1 + columns, columns)


def pick_kernel(colours, state, obs, place, *refs):
    outs, scratch = refs[:-1], refs[-1]
    tiles = len(outs)
    tile_rows = state.shape[0]
    columns, size = obs.shape
    share = size // tiles
    col, tile = place[0, 0], place[0, 1]
    bands = tiles if scratch.dtype == F32 else 1
    band = state.shape[1] // bands
    for n, colour in enumerate(colours):
        slot, active, batch = standing(col, colour, columns)
        first = jnp.where(active, (slot * tiles + tile) * tile_rows, -(1 << 20))
        local = obs[pl.ds(batch, 1), :] - first
        row = lax.broadcasted_iota(jnp.int32, (size, size), 0)
        same = row == lax.broadcasted_iota(jnp.int32, (size, size), 1)
        wanted = jnp.sum(jnp.where(same, local.astype(F32), 0.0), axis=1, keepdims=True)
        spots = lax.broadcasted_iota(jnp.int32, (size, tile_rows), 1)
        chosen = jnp.where(spots == wanted.astype(jnp.int32), 1.0, 0.0).astype(BF16)

        def pick_band(m, _):
            lanes = pl.ds(pl.multiple_of(m * band, band), band)
            rest = state[:, lanes]
            high = rest.astype(BF16)
            picked = dot(chosen, high)
            if scratch.dtype == F32:
                rest = rest - high.astype(F32)
                middle = rest.astype(BF16)
                picked = picked + dot(chosen, middle)
                picked = picked + dot(chosen, (rest - middle.astype(F32)).astype(BF16))
            scratch[:, lanes] = picked.astype(scratch.dtype)
            return 0

        lax.fori_loop(0, bands, pick_band, 0)
        for step, out in enumerate(outs):
            start = pl.multiple_of(lax.rem(tile + step, tiles) * share, share)
            out[n * share : (n + 1) * share, :] = scratch[pl.ds(start, share), :]


def setup_kernel(pairs, tiles, tile_rows, obs, levels, place, own, *outs):
    columns, size = obs.shape
    share = size // tiles
    col, tile = place[0, 0], place[0, 1]
    members = place[0, 2].astype(F32)
    lane = lax.broadcasted_iota(jnp.int32, (share, size), 1)
    mine = lane == lax.broadcasted_iota(jnp.int32, (share, size), 0) + tile * share

    def factor(source, which):
        slot, active, batch = standing(col, source, columns)
        level = levels[batch, slot * tiles + which].astype(F32) / 3.0
        return jnp.where(active, level, 0.0)

    for (targets, source), out in zip(pairs, outs):
        for n, target in enumerate(targets):
            slot, _, batch = standing(col, target, columns)
            inside = obs[pl.ds(batch, 1), :] - slot * (tiles * tile_rows)
            row = jnp.zeros((1, size), F32)
            for which in range(tiles):
                hit = (inside >= which * tile_rows) & (inside < (which + 1) * tile_rows)
                row = jnp.where(hit, factor(source, which), row)
            column = jnp.sum(jnp.where(mine, row, 0.0), axis=1, keepdims=True)
            out[n * share : (n + 1) * share, :] = column / members
    for colour in range(NCOL):
        outs[len(pairs) + colour][...] = jnp.full((1, 1), factor(colour, tile)) / members
    pieces = [own[:, n * share : (n + 1) * share] for n in range(tiles)]
    ordered = []
    for step in range(tiles):
        source = lax.rem(tile + tiles - step, tiles)
        piece = pieces[0]
        for n in range(1, tiles):
            piece = jnp.where(source == n, pieces[n], piece)
        ordered.append(piece)
    rest = jnp.concatenate(ordered, axis=1)
    row = lax.broadcasted_iota(jnp.int32, (EXTRA, size), 0)
    block = jnp.zeros((EXTRA, size), F32)
    for n in range(3):
        part = rest.astype(BF16).astype(F32)
        rest = rest - part
        block = jnp.where(row == n, part, block)
    for colour in range(NCOL):
        offset = lax.rem(col + (NCOL - colour), NCOL)
        sent = (offset == 0) | (offset == 2)
        out = outs[len(pairs) + NCOL + colour]
        out[...] = jnp.zeros(out.shape, BF16)
        out[:, :size] = jnp.where(sent, block, 0.0).astype(BF16)


def root_kernel(*refs):
    *pieces, variance, out = refs
    observed = jnp.concatenate([piece[...] for piece in pieces], axis=0)
    size, members = observed.shape
    row = lax.broadcasted_iota(jnp.int32, (size, size), 0)
    column = lax.broadcasted_iota(jnp.int32, (size, size), 1)
    eye = jnp.where(row == column, 1.0, 0.0).astype(F32)
    gram = dot_nt(observed, observed) / (members - 1) + eye * variance[...]
    trace = jnp.sum(jnp.sum(gram * eye, axis=1, keepdims=True), axis=0, keepdims=True)
    left = gram / trace
    right_h = halves(1.5 * eye - 0.5 * left)
    left_h = halves(mat_prod(halves(left), right_h))

    def next_term(left_h, right_h):
        return halves(1.5 * eye - 0.5 * mat_prod(right_h, left_h))

    def step(_, pair):
        left_h, right_h = pair
        term_h = next_term(left_h, right_h)
        return halves(mat_prod(left_h, term_h)), halves(mat_prod(term_h, right_h))

    left_h, right_h = lax.fori_loop(1, NS_STEPS - 1, step, (left_h, right_h))
    right = mat_prod(next_term(left_h, right_h), right_h)
    inverse_half = (right / jnp.sqrt(trace)).astype(BF16)
    out[...] = dot(inverse_half, observed).astype(BF16)


def summed(parts):
    total = parts[0][...]
    for part in parts[1:]:
        total = total + part[...]
    return total


def rows_kernel(count, *refs):
    *pairs, extra, out = refs[count:]
    rows = summed(refs[:count])
    for transformed, factor in zip(pairs[::2], pairs[1::2]):
        source = transformed[...]
        projected = dot_nt(rows.astype(BF16), source).astype(BF16)
        rows = rows - factor[...] * dot(projected, source)
    out[: rows.shape[0], :] = rows.astype(out.dtype)
    out[rows.shape[0] :, :] = extra[...]


def tile_kernel(state, transformed, factor, out):
    value = state[...]
    source = transformed[...]
    projected = dot_nt(value.astype(BF16), source).astype(BF16)
    out[...] = value - factor[...] * dot(projected, source)


def start_kernel(*refs):
    *parts, extra, out = refs
    rows = parts[0].shape[0]
    out[:rows, :] = summed(parts)
    out[rows:, :] = extra[...]


def join_kernel(*refs):
    *parts, whole, variance = refs
    total = summed(parts)
    rows, size = whole.shape[0], variance.shape[1]
    whole[...] = total[:rows]
    carried = total[rows:, :size].astype(F32)
    row = lax.broadcasted_iota(jnp.int32, carried.shape, 0)
    high, middle, low = (
        jnp.sum(jnp.where(row == n, carried, 0.0), axis=0, keepdims=True) for n in range(3)
    )
    variance[...] = (high + middle) + low


def on_device(anomalies, obs_rows, obs_var, taper_level):
    tile_rows, members = anomalies.shape
    batches, size = obs_rows.shape
    columns = lax.axis_size("gx")
    tiles = lax.axis_size("gy")
    share = size // tiles
    col = lax.axis_index("gx")
    tile = lax.axis_index("gy")
    place = jnp.stack([col, tile, jnp.int32(members - 1)]).astype(jnp.int32).reshape(1, 3)
    levels = taper_level.reshape(batches, 3 * tiles)
    everywhere = list(range(columns))

    def hop(value, pairs):
        flat = [
            ((a % columns) * tiles + b % tiles, (c % columns) * tiles + d % tiles)
            for (a, b), (c, d) in pairs
        ]
        return lax.ppermute(value, AXES, flat)

    def along_gy(value, step):
        return hop(value, [((c, n), (c, n + step)) for c in everywhere for n in range(tiles)])

    def along_gx(value, colour, step):
        trio = (-1, 0, 1)
        pairs = [
            ((b + trio[m], n), (b + trio[(m + step) % 3], n))
            for b in range(colour, columns, NCOL)
            for m in range(3)
            for n in range(tiles)
        ]
        pairs += [
            ((b + 2, n), (b + 2, n + 1 - 2 * (n % 2)))
            for b in range(colour, columns, NCOL)
            for n in range(tiles)
        ]
        return hop(value, pairs)

    def pick(colours, dtype, state):
        shape = jax.ShapeDtypeStruct((len(colours) * share, members), dtype)
        return kernel_call(
            functools.partial(pick_kernel, colours),
            [shape] * tiles,
            [state, obs_rows, place],
            "pick",
            2 * size * tile_rows * members * len(colours) * (1 if dtype == BF16 else 3),
            smem=(2,),
            scratch=[pltpu.VMEM((size, members), dtype)],
        )

    def scattered(parts):
        return [parts[0], *[along_gy(parts[n], n) for n in range(1, tiles)]]

    def joined(rows, colour, beside_it):
        first, second = (along_gx(rows, colour, step) for step in (1, 2))
        second, beside_it = lax.optimization_barrier((second, beside_it))
        shapes = [
            jax.ShapeDtypeStruct((share, members), BF16),
            jax.ShapeDtypeStruct((1, size), F32),
        ]
        args = [rows, first, second]
        return *kernel_call(join_kernel, shapes, args, "join", 1_000_000), beside_it

    def spread(whole):
        return [whole, *[along_gy(whole, step) for step in range(1, tiles)]]

    def transform(pieces, variance):
        return kernel_call(
            root_kernel,
            jax.ShapeDtypeStruct((size, members), BF16),
            [*pieces, variance],
            "root",
            8_000_000_000,
        )

    def move_tile(state, transformed, factor, blocks):
        some = pl.BlockSpec((tile_rows // blocks, members), lambda n: (n, 0))
        return pl.pallas_call(
            tile_kernel,
            out_shape=jax.ShapeDtypeStruct(state.shape, F32),
            grid=(blocks,),
            in_specs=[
                some,
                pl.BlockSpec((size, members), lambda n: (0, 0)),
                pl.BlockSpec((1, 1), lambda n: (0, 0)),
            ],
            out_specs=some,
            name="tile",
            interpret=INTERPRET,
            cost_estimate=pl.CostEstimate(
                flops=4 * tile_rows * size * members,
                bytes_accessed=2 * state.size * 4,
                transcendentals=0,
            ),
            compiler_params=pltpu.CompilerParams(vmem_limit_bytes=VMEM_LIMIT),
        )(state, transformed, factor)

    def move(parts, sources, extra):
        rows = share
        return kernel_call(
            functools.partial(rows_kernel, len(parts)),
            jax.ShapeDtypeStruct((rows + EXTRA, members), BF16),
            [*parts, *[ref for pair in sources for ref in pair], extra],
            "rows",
            4 * rows * size * members * len(sources),
        )

    parts = scattered(pick((0,), BF16, anomalies))
    picked = [None, *[pick((colour,), F32, anomalies) for colour in range(1, NCOL)]]
    pairs = [((target,), source) for target in range(1, NCOL) for source in range(target)]
    prepared = kernel_call(
        functools.partial(setup_kernel, pairs, tiles, tile_rows),
        [jax.ShapeDtypeStruct((len(t) * share, 1), F32) for t, _ in pairs]
        + [jax.ShapeDtypeStruct((1, 1), F32)] * NCOL
        + [jax.ShapeDtypeStruct((EXTRA, members), BF16)] * NCOL,
        [obs_rows, levels, place, obs_var],
        "setup",
        1_000_000,
        smem=(1, 2),
    )
    row_factor = {(t[0], source): out for (t, source), out in zip(pairs, prepared)}
    tile_factor = prepared[len(pairs) : len(pairs) + NCOL]
    extra = prepared[len(pairs) + NCOL :]
    parts[-1], picked[1] = lax.optimization_barrier((parts[-1], picked[1]))
    rows = kernel_call(
        start_kernel,
        jax.ShapeDtypeStruct((share + EXTRA, members), BF16),
        [*parts, extra[0]],
        "start",
        1_000_000,
    )

    state = anomalies
    done = []
    for colour in range(NCOL):
        if colour == 0:
            whole, variance, picked[2:] = joined(rows, colour, picked[2:])
        else:
            whole, variance, state = joined(rows, colour, state)
        pieces = spread(whole)
        if colour < NCOL - 1:
            coming, _ = lax.optimization_barrier((picked[colour + 1], whole))
            parts = scattered(coming)
        done.append(transform(pieces, variance))
        if colour < NCOL - 1:
            sources = [(done[n], row_factor[colour + 1, n]) for n in range(colour + 1)]
            rows = move(parts, sources, extra[colour + 1])
        blocks = 2 if colour < NCOL - 1 else LAST_BLOCKS
        state = move_tile(state, done[colour], tile_factor[colour], blocks)
    return state


def solution(mesh):
    in_specs = (P(AXES, None), P(), P("gx", None), P())
    return jax.shard_map(
        on_device,
        mesh=mesh,
        in_specs=in_specs,
        out_specs=P(AXES, None),
        check_vma=False,
    )
```

```python
import functools

import jax
import jax.numpy as jnp
from jax import lax
from jax.experimental import pallas as pl
from jax.experimental.pallas import tpu as pltpu
from jax.sharding import PartitionSpec as P

NCOL = 4
NS_STEPS = 12
AXES = ("gx", "gy")
VMEM_LIMIT = 20 << 20
LAST_BLOCKS = 1
EXTRA = 16
INTERPRET = False
F32 = jnp.float32
BF16 = jnp.bfloat16


def kernel_call(body, out, args, name, flops, smem=(), scratch=()):
    whole = pl.BlockSpec(memory_space=pltpu.VMEM)
    scalar = pl.BlockSpec(memory_space=pltpu.SMEM)
    leaves = [*args, *jax.tree.leaves(out)]
    return pl.pallas_call(
        body,
        out_shape=out,
        in_specs=[scalar if n in smem else whole for n in range(len(args))],
        out_specs=jax.tree.map(lambda _: whole, out),
        scratch_shapes=scratch,
        name=name,
        interpret=INTERPRET,
        cost_estimate=pl.CostEstimate(
            flops=flops,
            bytes_accessed=sum(leaf.size * leaf.dtype.itemsize for leaf in leaves),
            transcendentals=0,
        ),
        compiler_params=pltpu.CompilerParams(vmem_limit_bytes=VMEM_LIMIT),
    )(*args)


def dot(left, right):
    return jnp.dot(left, right, preferred_element_type=F32)


def dot_nt(left, right):
    return lax.dot_general(
        left, right, (((1,), (1,)), ((), ())), preferred_element_type=F32
    )


def halves(value):
    high = value.astype(BF16)
    return high, (value - high.astype(F32)).astype(BF16)


def mat_prod(left, right):
    return dot(left[0], right[0]) + (dot(left[0], right[1]) + dot(left[1], right[0]))


def standing(col, colour, columns):
    offset = lax.rem(col + (NCOL - colour), NCOL)
    slot = jnp.where(offset == 1, 2, jnp.where(offset == 3, 0, 1))
    return slot, offset != 2, lax.rem(col - slot + 1 + columns, columns)


def pick_kernel(colours, state, obs, place, *refs):
    outs, scratch = refs[:-1], refs[-1]
    tiles = len(outs)
    tile_rows = state.shape[0]
    columns, size = obs.shape
    share = size // tiles
    col, tile = place[0, 0], place[0, 1]
    bands = tiles if scratch.dtype == F32 else 1
    band = state.shape[1] // bands
    for n, colour in enumerate(colours):
        slot, active, batch = standing(col, colour, columns)
        first = jnp.where(active, (slot * tiles + tile) * tile_rows, -(1 << 20))
        local = obs[pl.ds(batch, 1), :] - first
        row = lax.broadcasted_iota(jnp.int32, (size, size), 0)
        same = row == lax.broadcasted_iota(jnp.int32, (size, size), 1)
        wanted = jnp.sum(jnp.where(same, local.astype(F32), 0.0), axis=1, keepdims=True)
        spots = lax.broadcasted_iota(jnp.int32, (size, tile_rows), 1)
        chosen = jnp.where(spots == wanted.astype(jnp.int32), 1.0, 0.0).astype(BF16)

        def pick_band(m, _):
            lanes = pl.ds(pl.multiple_of(m * band, band), band)
            rest = state[:, lanes]
            high = rest.astype(BF16)
            picked = dot(chosen, high)
            if scratch.dtype == F32:
                rest = rest - high.astype(F32)
                middle = rest.astype(BF16)
                picked = picked + dot(chosen, middle)
                picked = picked + dot(chosen, (rest - middle.astype(F32)).astype(BF16))
            scratch[:, lanes] = picked.astype(scratch.dtype)
            return 0

        lax.fori_loop(0, bands, pick_band, 0)
        for step, out in enumerate(outs):
            start = pl.multiple_of(lax.rem(tile + step, tiles) * share, share)
            out[n * share : (n + 1) * share, :] = scratch[pl.ds(start, share), :]


def setup_kernel(pairs, tiles, tile_rows, obs, levels, place, own, *outs):
    columns, size = obs.shape
    share = size // tiles
    col, tile = place[0, 0], place[0, 1]
    members = place[0, 2].astype(F32)
    lane = lax.broadcasted_iota(jnp.int32, (share, size), 1)
    mine = lane == lax.broadcasted_iota(jnp.int32, (share, size), 0) + tile * share

    def factor(source, which):
        slot, active, batch = standing(col, source, columns)
        level = levels[batch, slot * tiles + which].astype(F32) / 3.0
        return jnp.where(active, level, 0.0)

    for (targets, source), out in zip(pairs, outs):
        for n, target in enumerate(targets):
            slot, _, batch = standing(col, target, columns)
            inside = obs[pl.ds(batch, 1), :] - slot * (tiles * tile_rows)
            row = jnp.zeros((1, size), F32)
            for which in range(tiles):
                hit = (inside >= which * tile_rows) & (inside < (which + 1) * tile_rows)
                row = jnp.where(hit, factor(source, which), row)
            column = jnp.sum(jnp.where(mine, row, 0.0), axis=1, keepdims=True)
            out[n * share : (n + 1) * share, :] = column / members
    for colour in range(NCOL):
        outs[len(pairs) + colour][...] = jnp.full((1, 1), factor(colour, tile)) / members
    pieces = [own[:, n * share : (n + 1) * share] for n in range(tiles)]
    ordered = []
    for step in range(tiles):
        source = lax.rem(tile + tiles - step, tiles)
        piece = pieces[0]
        for n in range(1, tiles):
            piece = jnp.where(source == n, pieces[n], piece)
        ordered.append(piece)
    rest = jnp.concatenate(ordered, axis=1)
    row = lax.broadcasted_iota(jnp.int32, (EXTRA, size), 0)
    block = jnp.zeros((EXTRA, size), F32)
    for n in range(3):
        part = rest.astype(BF16).astype(F32)
        rest = rest - part
        block = jnp.where(row == n, part, block)
    for colour in range(NCOL):
        offset = lax.rem(col + (NCOL - colour), NCOL)
        sent = (offset == 0) | (offset == 2)
        out = outs[len(pairs) + NCOL + colour]
        out[...] = jnp.zeros(out.shape, BF16)
        out[:, :size] = jnp.where(sent, block, 0.0).astype(BF16)


def root_kernel(*refs):
    *pieces, variance, out = refs
    observed = jnp.concatenate([piece[...] for piece in pieces], axis=0)
    size, members = observed.shape
    row = lax.broadcasted_iota(jnp.int32, (size, size), 0)
    column = lax.broadcasted_iota(jnp.int32, (size, size), 1)
    eye = jnp.where(row == column, 1.0, 0.0).astype(F32)
    gram = dot_nt(observed, observed) / (members - 1) + eye * variance[...]
    trace = jnp.sum(jnp.sum(gram * eye, axis=1, keepdims=True), axis=0, keepdims=True)
    left = gram / trace
    right_h = halves(1.5 * eye - 0.5 * left)
    left_h = halves(mat_prod(halves(left), right_h))

    def next_term(left_h, right_h):
        return halves(1.5 * eye - 0.5 * mat_prod(right_h, left_h))

    def step(_, pair):
        left_h, right_h = pair
        term_h = next_term(left_h, right_h)
        return halves(mat_prod(left_h, term_h)), halves(mat_prod(term_h, right_h))

    left_h, right_h = lax.fori_loop(1, NS_STEPS - 1, step, (left_h, right_h))
    right = mat_prod(next_term(left_h, right_h), right_h)
    inverse_half = (right / jnp.sqrt(trace)).astype(BF16)
    out[...] = dot(inverse_half, observed).astype(BF16)


def summed(parts):
    total = parts[0][...]
    for part in parts[1:]:
        total = total + part[...]
    return total


def rows_kernel(count, *refs):
    *pairs, extra, out = refs[count:]
    rows = summed(refs[:count])
    for transformed, factor in zip(pairs[::2], pairs[1::2]):
        source = transformed[...]
        projected = dot_nt(rows.astype(BF16), source).astype(BF16)
        rows = rows - factor[...] * dot(projected, source)
    out[: rows.shape[0], :] = rows.astype(out.dtype)
    out[rows.shape[0] :, :] = extra[...]


def tile_kernel(state, transformed, factor, out):
    value = state[...]
    source = transformed[...]
    projected = dot_nt(value.astype(BF16), source).astype(BF16)
    out[...] = value - factor[...] * dot(projected, source)


def start_kernel(*refs):
    *parts, extra, out = refs
    rows = parts[0].shape[0]
    out[:rows, :] = summed(parts)
    out[rows:, :] = extra[...]


def join_kernel(*refs):
    *parts, whole, variance = refs
    total = summed(parts)
    rows, size = whole.shape[0], variance.shape[1]
    whole[...] = total[:rows]
    carried = total[rows:, :size].astype(F32)
    row = lax.broadcasted_iota(jnp.int32, carried.shape, 0)
    high, middle, low = (
        jnp.sum(jnp.where(row == n, carried, 0.0), axis=0, keepdims=True) for n in range(3)
    )
    variance[...] = (high + middle) + low


def on_device(anomalies, obs_rows, obs_var, taper_level):
    tile_rows, members = anomalies.shape
    batches, size = obs_rows.shape
    columns = lax.axis_size("gx")
    tiles = lax.axis_size("gy")
    share = size // tiles
    col = lax.axis_index("gx")
    tile = lax.axis_index("gy")
    place = jnp.stack([col, tile, jnp.int32(members - 1)]).astype(jnp.int32).reshape(1, 3)
    levels = taper_level.reshape(batches, 3 * tiles)
    everywhere = list(range(columns))

    def hop(value, pairs):
        flat = [
            ((a % columns) * tiles + b % tiles, (c % columns) * tiles + d % tiles)
            for (a, b), (c, d) in pairs
        ]
        return lax.ppermute(value, AXES, flat)

    def along_gy(value, step):
        return hop(value, [((c, n), (c, n + step)) for c in everywhere for n in range(tiles)])

    def along_gx(value, colour, step):
        trio = (-1, 0, 1)
        pairs = [
            ((b + trio[m], n), (b + trio[(m + step) % 3], n))
            for b in range(colour, columns, NCOL)
            for m in range(3)
            for n in range(tiles)
        ]
        pairs += [
            ((b + 2, n), (b + 2, n + 1 - 2 * (n % 2)))
            for b in range(colour, columns, NCOL)
            for n in range(tiles)
        ]
        return hop(value, pairs)

    def pick(colours, dtype, state):
        shape = jax.ShapeDtypeStruct((len(colours) * share, members), dtype)
        return kernel_call(
            functools.partial(pick_kernel, colours),
            [shape] * tiles,
            [state, obs_rows, place],
            "pick",
            2 * size * tile_rows * members * len(colours) * (1 if dtype == BF16 else 3),
            smem=(2,),
            scratch=[pltpu.VMEM((size, members), dtype)],
        )

    def scattered(parts):
        return [parts[0], *[along_gy(parts[n], n) for n in range(1, tiles)]]

    def joined(rows, colour, beside_it):
        first, second = (along_gx(rows, colour, step) for step in (1, 2))
        second, beside_it = lax.optimization_barrier((second, beside_it))
        shapes = [
            jax.ShapeDtypeStruct((share, members), BF16),
            jax.ShapeDtypeStruct((1, size), F32),
        ]
        args = [rows, first, second]
        return *kernel_call(join_kernel, shapes, args, "join", 1_000_000), beside_it

    def spread(whole):
        return [whole, *[along_gy(whole, step) for step in range(1, tiles)]]

    def transform(pieces, variance):
        return kernel_call(
            root_kernel,
            jax.ShapeDtypeStruct((size, members), BF16),
            [*pieces, variance],
            "root",
            8_000_000_000,
        )

    def move_tile(state, transformed, factor, blocks):
        some = pl.BlockSpec((tile_rows // blocks, members), lambda n: (n, 0))
        return pl.pallas_call(
            tile_kernel,
            out_shape=jax.ShapeDtypeStruct(state.shape, F32),
            grid=(blocks,),
            in_specs=[
                some,
                pl.BlockSpec((size, members), lambda n: (0, 0)),
                pl.BlockSpec((1, 1), lambda n: (0, 0)),
            ],
            out_specs=some,
            name="tile",
            interpret=INTERPRET,
            cost_estimate=pl.CostEstimate(
                flops=4 * tile_rows * size * members,
                bytes_accessed=2 * state.size * 4,
                transcendentals=0,
            ),
            compiler_params=pltpu.CompilerParams(vmem_limit_bytes=VMEM_LIMIT),
        )(state, transformed, factor)

    def move(parts, sources, extra):
        rows = share
        return kernel_call(
            functools.partial(rows_kernel, len(parts)),
            jax.ShapeDtypeStruct((rows + EXTRA, members), BF16),
            [*parts, *[ref for pair in sources for ref in pair], extra],
            "rows",
            4 * rows * size * members * len(sources),
        )

    parts = scattered(pick((0,), BF16, anomalies))
    picked = [None, *[pick((colour,), F32, anomalies) for colour in range(1, NCOL)]]
    pairs = [((target,), source) for target in range(1, NCOL) for source in range(target)]
    prepared = kernel_call(
        functools.partial(setup_kernel, pairs, tiles, tile_rows),
        [jax.ShapeDtypeStruct((len(t) * share, 1), F32) for t, _ in pairs]
        + [jax.ShapeDtypeStruct((1, 1), F32)] * NCOL
        + [jax.ShapeDtypeStruct((EXTRA, members), BF16)] * NCOL,
        [obs_rows, levels, place, obs_var],
        "setup",
        1_000_000,
        smem=(1, 2),
    )
    row_factor = {(t[0], source): out for (t, source), out in zip(pairs, prepared)}
    tile_factor = prepared[len(pairs) : len(pairs) + NCOL]
    extra = prepared[len(pairs) + NCOL :]
    parts[-1], picked[1:3] = lax.optimization_barrier((parts[-1], picked[1:3]))
    rows = kernel_call(
        start_kernel,
        jax.ShapeDtypeStruct((share + EXTRA, members), BF16),
        [*parts, extra[0]],
        "start",
        1_000_000,
    )

    state = anomalies
    done = []
    for colour in range(NCOL):
        if colour == 0:
            whole, variance, picked[3:] = joined(rows, colour, picked[3:])
        else:
            whole, variance, state = joined(rows, colour, state)
        pieces = spread(whole)
        if colour < NCOL - 1:
            coming, _ = lax.optimization_barrier((picked[colour + 1], whole))
            parts = scattered(coming)
        done.append(transform(pieces, variance))
        if colour < NCOL - 1:
            sources = [(done[n], row_factor[colour + 1, n]) for n in range(colour + 1)]
            rows = move(parts, sources, extra[colour + 1])
        blocks = 2 if colour < NCOL - 1 else LAST_BLOCKS
        state = move_tile(state, done[colour], tile_factor[colour], blocks)
    return state


def solution(mesh):
    in_specs = (P(AXES, None), P(), P("gx", None), P())
    return jax.shard_map(
        on_device,
        mesh=mesh,
        in_specs=in_specs,
        out_specs=P(AXES, None),
        check_vma=False,
    )
```
